256 devices in a mesh: wide: 8 (over x_lo, y), narrow: 32 (over z, x_hi, core).
Axes of the slice: x: 4 (x_hi: 2, x_lo: 2; x = x_hi * 2 + x_lo), y: 4, z: 8, core: 2. Of those that a mesh axis runs over, the one named last changes fastest.
Arguments:
- right_side: float32 [1024, 320, 128], P(('wide', 'narrow')), may hold values from -6 to 6
- fine_blocks: float32 [1024, 320, 320], P(('wide', 'narrow'))
- fine_inverses: float32 [1024, 320, 320], P(('wide', 'narrow')), as said below
- fine_lifts: float32 [6, 320, 80], replicated, may hold values from -0.625 to 0.625
- fine_coefs: float32 [1024, 6, 80], P(('wide', 'narrow')), may hold values from 0.1 to 0.4
- coarse_blocks: float32 [1024, 40, 40], P(('wide', 'narrow'))
- coarse_inverses: float32 [1024, 40, 40], P(('wide', 'narrow')), as said below
- coarse_lifts: float32 [6, 40, 20], replicated, may hold values from -1.25 to 1.25
- coarse_coefs: float32 [1024, 6, 20], P(('wide', 'narrow')), may hold values from 0.15 to 0.6
- neighbours: int32 [1024, 6], P(('wide', 'narrow')), may hold values from -1 to 1023, as said below
- counts: int32 [256], P(('wide', 'narrow')), may hold values from 2 to 4, as said below
Outputs:
- solution: float32 [1024, 320, 128], P(('wide', 'narrow'))
The draws below stay inside these ranges and needn't reach their ends.
Inputs may be any that keep to these rules, and one draw needn't show every extreme that they name: Slots 0 to counts - 1 of a device are its live elements, the rest are empty. Some device has all 4 slots live and some has only 2. Each entry is -1 or the index of a live element; empty slots hold -1 on all faces. If neighbours[e, f] = g then neighbours[g, f xor 1] = e. Across faces 0 and 1 the neighbour lies on the same device or on the device one wide index lower (face 0) or higher (face 1) with the same narrow index; across faces 2 and 3 likewise along narrow; across faces 4 and 5 on the same device. For every pair of devices next to each other along either axis exactly 1 face crosses between them. `fine_inverses`: an approximate inverse of the element's fine block, as incomplete factors give it. `coarse_inverses`: an approximate inverse of the element's coarse block, as incomplete factors give it.
All inputs are finite; a program needn't handle non-finite values.
Results may differ from the reference program's by a relative error of at most 0.00022.
Values sent between devices are 32-bit elements; how exact they have to be, the bound alone decides.
A program may use at most 64 MiB of HBM per device.

```python
import math
import jax
import jax.numpy as jnp
import numpy as np
from jax import lax

NVAR = 5
NODE1 = 4
NF = 320
NFACE = 80
NC = 40
NCF = 20
E_DEV = 4
RHS = 128
PRE_SWEEPS = 2
POST_SWEEPS = 2
COARSE_SWEEPS = 4
NE = 1024
N_WIDE = 8
N_NARROW = 32


def block_pair(base_key, elements, order):
    diag_key = jax.random.fold_in(base_key, 301)
    coupling_key = jax.random.fold_in(base_key, 302)
    noise_key = jax.random.fold_in(base_key, 303)
    diagonal = jnp.exp(jax.random.uniform(diag_key, (elements, order), jnp.float32, 0.0, 0.6931))
    coupling = jax.random.normal(coupling_key, (elements, order, order), jnp.float32) * (0.3 / np.sqrt(order))
    identity = jnp.eye(order, dtype=jnp.float32)
    blocks = diagonal[:, :, None] * identity + coupling
    reciprocal = 1.0 / diagonal
    approximate = reciprocal[:, :, None] * identity - reciprocal[:, :, None] * coupling * reciprocal[:, None, :]
    noise = jax.random.normal(noise_key, (elements, order, order), jnp.float32) * (0.02 / np.sqrt(order))
    return (blocks, approximate + noise)


def bounded_perm(base_key, length):
    shuffled = jax.random.permutation(base_key, E_DEV)
    places = jnp.arange(E_DEV)
    ordering = jnp.argsort(jnp.where(shuffled < length, places, E_DEV + places))
    result = shuffled[ordering]
    return (result, jnp.argsort(result))


def axis_faces(device_ids, places, counts, forward, backward, local_perm, local_inv, step_size, position, extent, devices):
    crossing = E_DEV // 4
    rows_back = backward[jnp.clip(device_ids[:, 0] - step_size, 0, devices - 1)]
    plus_cross = places < crossing
    plus_cross_slot = crossing + jnp.take_along_axis(forward, jnp.clip(places + 0 * device_ids, 0, crossing - 1), axis=1)
    plus_local_k = jnp.take_along_axis(local_perm, jnp.clip(places - crossing + 0 * device_ids, 0, E_DEV - 1), axis=1)
    plus_local_slot = jnp.where(plus_local_k < crossing, plus_local_k, plus_local_k + crossing)
    plus_dev = jnp.where(plus_cross, device_ids + step_size, device_ids)
    plus_slot = jnp.where(plus_cross, plus_cross_slot, plus_local_slot)
    plus_ok = jnp.where(plus_cross, position < extent - 1, places < counts[:, None])
    minus_cross = jnp.logical_and(places >= crossing, places < 2 * crossing)
    minus_cross_slot = jnp.take_along_axis(rows_back, jnp.clip(places - crossing + 0 * device_ids, 0, crossing - 1), axis=1)
    minus_local_k = jnp.where(places < crossing, places, places - crossing) + 0 * device_ids
    minus_local_slot = crossing + jnp.take_along_axis(local_inv, jnp.clip(minus_local_k, 0, E_DEV - 1), axis=1)
    minus_dev = jnp.where(minus_cross, device_ids - step_size, device_ids)
    minus_slot = jnp.where(minus_cross, minus_cross_slot, minus_local_slot)
    minus_ok = jnp.where(minus_cross, position > 0, places < counts[:, None])
    return ((minus_dev, minus_slot, minus_ok), (plus_dev, plus_slot, plus_ok))


def mesh_links(base_key):
    devices = N_WIDE * N_NARROW
    crossing = E_DEV // 4
    lowest = E_DEV // 2
    key_list = jax.random.split(jax.random.fold_in(base_key, 7), 9)
    counts = jax.random.randint(key_list[0], (devices,), lowest, E_DEV + 1)
    full_at = devices - 1
    least_at = (full_at + 1 + jax.random.randint(key_list[2], (), 0, devices - 1)) % devices
    counts = counts.at[least_at].set(lowest).at[full_at].set(E_DEV)

    def cross_perm(one_key):
        return jax.random.permutation(one_key, crossing)
    perm_wide = jax.vmap(cross_perm)(jax.random.split(key_list[3], devices))
    perm_narrow = jax.vmap(cross_perm)(jax.random.split(key_list[4], devices))
    inv_wide = jnp.argsort(perm_wide, axis=1)
    inv_narrow = jnp.argsort(perm_narrow, axis=1)
    free_length = counts - crossing
    local_wide, local_wide_inv = jax.vmap(bounded_perm)(jax.random.split(key_list[5], devices), free_length)
    local_narrow, local_narrow_inv = jax.vmap(bounded_perm)(jax.random.split(key_list[6], devices), free_length)
    local_depth, local_depth_inv = jax.vmap(bounded_perm)(jax.random.split(key_list[7], devices), counts)
    labels, labels_inv = jax.vmap(bounded_perm)(jax.random.split(key_list[8], devices), counts)
    device_ids = jnp.arange(devices)[:, None]
    places = jnp.arange(E_DEV)[None, :]
    wide_position = device_ids // N_NARROW
    narrow_position = device_ids % N_NARROW
    faces_wide = axis_faces(device_ids, places, counts, perm_wide, inv_wide, local_wide, local_wide_inv, N_NARROW, wide_position, N_WIDE, devices)
    faces_narrow = axis_faces(device_ids, places, counts, perm_narrow, inv_narrow, local_narrow, local_narrow_inv, 1, narrow_position, N_NARROW, devices)
    alive = places < counts[:, None]
    same_device = device_ids + 0 * places
    depth_minus = (same_device, local_depth_inv, alive)
    depth_plus = (same_device, local_depth, alive)
    pattern = [faces_wide[0], faces_wide[1], faces_narrow[0], faces_narrow[1], depth_minus, depth_plus]
    columns = []
    for face_side in range(6):
        face_dev, face_slot, face_ok = pattern[face_side]
        clip_dev = jnp.clip(face_dev, 0, devices - 1)
        clip_slot = jnp.clip(face_slot, 0, E_DEV - 1)
        global_ids = clip_dev * E_DEV + labels[clip_dev, clip_slot]
        global_ids = jnp.where(jnp.logical_and(face_ok, alive), global_ids, -1)
        moved = jnp.take_along_axis(global_ids, labels_inv, axis=1)
        moved = jnp.where(alive, moved, -1)
        columns.append(moved)
    table_all = jnp.stack(columns, axis=2).reshape(devices * E_DEV, 6).astype(jnp.int32)
    return (counts.astype(jnp.int32), table_all)


def draw_fine_blocks(key, part):
    return block_pair(jax.random.fold_in(key, 11), NE, NF)[0]


def draw_fine_inverses(key, part):
    return block_pair(jax.random.fold_in(key, 11), NE, NF)[1]


def draw_coarse_blocks(key, part):
    return block_pair(jax.random.fold_in(key, 12), NE, NC)[0]


def draw_coarse_inverses(key, part):
    return block_pair(jax.random.fold_in(key, 12), NE, NC)[1]


def draw_neighbours(key, part):
    return mesh_links(key)[1]


def draw_counts(key, part):
    return mesh_links(key)[0]


def block_levels(key, dims, cuts, low, largest):
    def one(dim, blocks):
        steps = jax.random.uniform(jax.random.fold_in(jax.random.fold_in(key, 6), dim), (blocks,), jnp.float32, low / len(cuts), largest / len(cuts))
        return jnp.repeat(jnp.exp(steps), dims[dim] // blocks).reshape((-1,) + (1,) * (len(dims) - dim - 1))

    loudness = one(*cuts[0])
    for cut in cuts[1:]:
        loudness = loudness * one(*cut)
    return loudness


def normal_values(key, shape, width, limit, shards=(), kind=jnp.bfloat16):
    gain = block_levels(key, shape, shards, -0.22, 0.18) if shards else 1.0
    entries = jax.random.normal(key, shape, jnp.float32) * width * gain
    return jnp.minimum(jnp.maximum(entries, -limit), limit).astype(kind)


def setup_inputs(seed: int = 0) -> dict:
    key_of = jax.random.split(jax.random.key(seed), 12)
    right_side = normal_values(key_of[0], (NE, NF, RHS), 1.0, 6.0, ((0, 256),), jnp.float32)
    fine_blocks = draw_fine_blocks(jax.random.fold_in(key_of[11], 71), 0)
    fine_inverses = draw_fine_inverses(jax.random.fold_in(key_of[11], 71), 0)
    fine_lifts = normal_values(key_of[3], (6, NF, NFACE), NFACE ** -0.5, 0.625, (), jnp.float32)
    fine_coefs = jnp.clip(jnp.exp(math.log(0.4) - 1.3862944 * jax.random.uniform(key_of[4], (NE, 6, NFACE), jnp.float32) ** block_levels(key_of[4], (NE, 6, NFACE), ((0, 256),), -0.2, 0.2)), 0.1, 0.4)
    coarse_blocks = draw_coarse_blocks(jax.random.fold_in(key_of[11], 71), 0)
    coarse_inverses = draw_coarse_inverses(jax.random.fold_in(key_of[11], 71), 0)
    coarse_lifts = normal_values(key_of[7], (6, NC, NCF), NCF ** -0.5, 1.25, (), jnp.float32)
    coarse_coefs = jnp.clip(jnp.exp(math.log(0.6) - 1.3862944 * jax.random.uniform(key_of[8], (NE, 6, NCF), jnp.float32) ** block_levels(key_of[8], (NE, 6, NCF), ((0, 256),), -0.2, 0.2)), 0.15, 0.6)
    neighbours = draw_neighbours(jax.random.fold_in(key_of[11], 71), 0)
    counts = draw_counts(jax.random.fold_in(key_of[11], 71), 0)
    return {"right_side": right_side, "fine_blocks": fine_blocks, "fine_inverses": fine_inverses, "fine_lifts": fine_lifts, "fine_coefs": fine_coefs, "coarse_blocks": coarse_blocks, "coarse_inverses": coarse_inverses, "coarse_lifts": coarse_lifts, "coarse_coefs": coarse_coefs, "neighbours": neighbours, "counts": counts}


damping = 0.8
highest = lax.Precision.HIGHEST

def face_rows(node_count, variables):
    cube_size = node_count * node_count * node_count
    lattice = np.arange(cube_size).reshape(node_count, node_count, node_count)
    table_list = []
    for face_side in range(6):
        layer_index = 0 if face_side % 2 == 0 else node_count - 1
        direction = face_side // 2
        if direction == 0:
            layer = lattice[layer_index, :, :]
        elif direction == 1:
            layer = lattice[:, layer_index, :]
        else:
            layer = lattice[:, :, layer_index]
        nodes_on = layer.reshape(-1)
        table_list.append(np.concatenate([nodes_on + variable * cube_size for variable in range(variables)]))
    return np.stack(table_list).astype(np.int32)

def prolong_table(node_count, variables):
    if node_count == 4:
        points = np.array([-1.0, -1.0 / np.sqrt(5.0), 1.0 / np.sqrt(5.0), 1.0])
    else:
        points = np.linspace(-1.0, 1.0, node_count)
    linear = np.stack([(1.0 - points) / 2.0, (1.0 + points) / 2.0], axis=1)
    tensor_hat = linear[:, None, None, :, None, None] * linear[None, :, None, None, :, None] * linear[None, None, :, None, None, :]
    tensor_hat = tensor_hat.reshape(node_count * node_count * node_count, 8)
    return np.kron(np.eye(variables), tensor_hat).astype(np.float32)

def block_apply(blocks, vectors):
    return jnp.einsum('epq,eqr->epr', blocks, vectors, precision=highest)

def couple(state_field, neighbours, face_coefs, face_lifts, face_table):
    present = neighbours >= 0
    clipped = jnp.where(present, neighbours, 0)
    summed = jnp.zeros(state_field.shape, state_field.dtype)
    for face_side in range(6):
        traces = state_field[:, face_table[face_side ^ 1], :]
        nearby = jnp.where(present[:, face_side, None, None], traces[clipped[:, face_side]], 0.0)
        scaled = face_coefs[:, face_side, :, None] * nearby
        summed = summed + jnp.einsum('pq,eqr->epr', face_lifts[face_side], scaled, precision=highest)
    return summed

def sweep(solution, rhs_live, blocks, inverses, couple_fn):
    residual = rhs_live - block_apply(blocks, solution) - couple_fn(solution)
    return solution + damping * block_apply(inverses, residual)

def reference(right_side, fine_blocks, fine_inverses, fine_lifts, fine_coefs, coarse_blocks, coarse_inverses, coarse_lifts, coarse_coefs, neighbours, counts):
    elements = right_side.shape[0]
    places = jnp.arange(elements)
    live_mask = (places % E_DEV < counts[places // E_DEV]).astype(right_side.dtype)
    rhs_live = right_side * live_mask[:, None, None]
    fine_table = face_rows(NODE1, NVAR)
    coarse_table = face_rows(2, NVAR)
    prolong = jnp.asarray(prolong_table(NODE1, NVAR), right_side.dtype)

    def fine_couple(state_field):
        return couple(state_field, neighbours, fine_coefs, fine_lifts, fine_table)

    def coarse_couple(state_field):
        return couple(state_field, neighbours, coarse_coefs, coarse_lifts, coarse_table)
    solution = jnp.zeros(right_side.shape, right_side.dtype)
    for sweep_index in range(PRE_SWEEPS):
        solution = sweep(solution, rhs_live, fine_blocks, fine_inverses, fine_couple)
    residual = rhs_live - block_apply(fine_blocks, solution) - fine_couple(solution)
    coarse_rhs = 0.25 * jnp.einsum('pq,epr->eqr', prolong, residual, precision=highest)
    coarse_solution = jnp.zeros(coarse_rhs.shape, coarse_rhs.dtype)
    for sweep_index in range(COARSE_SWEEPS):
        coarse_solution = sweep(coarse_solution, coarse_rhs, coarse_blocks, coarse_inverses, coarse_couple)
    solution = solution + jnp.einsum('pq,eqr->epr', prolong, coarse_solution, precision=highest)
    for sweep_index in range(POST_SWEEPS):
        solution = sweep(solution, rhs_live, fine_blocks, fine_inverses, fine_couple)
    return solution
```

```python
import jax
import jax.numpy as jnp
import numpy as np
from jax import lax
from jax.experimental import pallas as pl
from jax.experimental.pallas import tpu as pltpu
from jax.sharding import PartitionSpec as P

NVAR = 5
SLOTS = 4
NF = 320
NFACE = 80
NC = 40
NCF = 20
HALO = 24
RHS = 128
WIDE = 8
NARROW = 32
MESH = pl.DeviceIdType.MESH
highest = lax.Precision.HIGHEST
bf16 = jnp.bfloat16
f32 = jnp.float32


def linear_table():
    points = np.array([-1.0, -1.0 / np.sqrt(5.0), 1.0 / np.sqrt(5.0), 1.0])
    return np.stack([(1.0 - points) / 2.0, (1.0 + points) / 2.0], axis=1)


def split_np(values):
    values = values.astype(np.float32)
    high = values.astype(bf16)
    low = (values - high.astype(np.float32)).astype(bf16)
    return high, low


def tables():
    linear = linear_table()
    cube = np.kron(np.kron(linear, linear), linear)
    prolong = np.kron(np.eye(NVAR), cube).astype(np.float32)
    flat = np.kron(np.eye(NVAR), np.kron(linear, linear)).astype(np.float32)
    high, low = split_np(prolong)
    lift = np.zeros((NF, 128), high.dtype)
    lift[:, :NC] = high
    lift[:, 64 : 64 + NC] = low
    wide_order = np.zeros((4, NFACE, HALO), np.float32)
    for face in range(4):
        for t in range(NCF):
            position = (t % 4) * 5 + t // 4 if face < 2 else (t % 2) * 10 + t // 2
            wide_order[face, :, position] = flat[:, t]
    face_tab = np.zeros((4, 256, 256), high.dtype)
    for face in range(4):
        high, low = split_np(wide_order[face])
        for start in (0, 128):
            face_tab[face, start : start + NFACE, :HALO] = high
            face_tab[face, start : start + NFACE, 128 : 128 + HALO] = low
    return lift, np.ascontiguousarray(prolong.T), face_tab


def halves(x):
    high = x.astype(bf16)
    low = (x - high.astype(f32)).astype(bf16)
    return high, low


def pack_left(x):
    high, low = halves(x)
    return jnp.concatenate(
        [high[:, :256], low[:, :256], jnp.concatenate([high[:, 256:], low[:, 256:]], axis=1)],
        axis=1,
    )


def pack_right(x):
    high, low = halves(x)
    both = jnp.concatenate([high, low], axis=1)
    main, rest = both[:256], both[256:]
    return jnp.concatenate([main, main, rest, rest], axis=0)


def product(left, right):
    out = jnp.dot(left, right, preferred_element_type=f32)
    return out[:, :128] + out[:, 128:]


def pad_rows(x, rows):
    return jnp.concatenate([x, jnp.zeros((rows - x.shape[0], x.shape[1]), x.dtype)], axis=0)


def pad_lanes(x, lanes):
    return jnp.concatenate([x, jnp.zeros((x.shape[0], lanes - x.shape[1]), x.dtype)], axis=1)


def twice(x, rows):
    high, low = halves(pad_rows(x, rows))
    both = jnp.concatenate([high, low], axis=1)
    return jnp.concatenate([both, both], axis=0)


def trace(ref, slot, face):
    odd = face & 1
    if face < 2:
        return jnp.concatenate(
            [ref[slot, pl.ds(64 * v + 48 * odd, 16), :] for v in range(NVAR)], axis=0
        )
    if face < 4:
        tiles = ref[slot].reshape(20, 16, RHS)[:, 8 * odd : 8 * odd + 8]
        pairs = tiles.reshape(10, 2, 8, RHS)
        first, second = pairs[:, 0], pairs[:, 1]
        upper = lax.broadcasted_iota(jnp.int32, (10, 8, RHS), 1) < 4
        if odd:
            out = jnp.where(upper, pltpu.roll(first, 4, 1), second)
        else:
            out = jnp.where(upper, first, pltpu.roll(second, 4, 1))
        return out.reshape(NFACE, RHS)
    return ref[slot, pl.ds(3 * odd, NFACE, stride=4), :]


def coarse_trace_to(ref, slot, face, out):
    odd = face & 1
    if face < 2:
        for q in range(4):
            out[pl.ds(5 * q, 5), :] = ref[slot, pl.ds(4 * odd + q, 5, stride=8), :]
    else:
        for q in range(2):
            out[pl.ds(10 * q, 10), :] = ref[slot, pl.ds(2 * odd + q, 10, stride=4), :]


def coarse_rows(face, t):
    odd = face & 1
    var = lax.shift_right_logical(t, 2)
    a = lax.shift_right_logical(t, 1) & 1
    b = t & 1
    if face < 2:
        return var * 8 + 4 * odd + a * 2 + b
    if face < 4:
        return var * 8 + a * 4 + 2 * odd + b
    return var * 8 + a * 4 + b * 2 + odd


def halo_rows(face, t):
    if face < 2:
        return (t & 3) * 5 + lax.shift_right_logical(t, 2)
    return (t & 1) * 10 + lax.shift_right_logical(t, 1)


def kernel(
    rhs_hbm, blocks_hbm, inv_hbm, lifts_hbm, coefs_hbm,
    cblocks_hbm, cinv_hbm, clifts_hbm, ccoefs_hbm, nbr, counts,
    lift_hbm, restrict_hbm, face_hbm,
    out,
    rhs, stage, inv_stage, lifts, coefs, cblocks, cinv, clifts, ccoefs, lift_tab, restrict_tab, face_tab,
    left_a, left_d, lift_h, lift_l, coef_cols, coef_sq,
    v, vpre, x_h, x_l, r_loc, cross_l, cross_g, cross_k, left_ip, coarse_m, w1, w,
    z_old, f_send, f_recv, c_send, c_recv,
    load_sem, send_sem, recv_sem,
):
    wide = lax.axis_index("wide")
    narrow = lax.axis_index("narrow")
    base = (wide * NARROW + narrow) * SLOTS
    sides = [
        (wide > 0, {"wide": wide - 1}),
        (wide < WIDE - 1, {"wide": wide + 1}),
        (narrow > 0, {"narrow": narrow - 1}),
        (narrow < NARROW - 1, {"narrow": narrow + 1}),
    ]

    loads = {}
    count = 0
    pairs = [("rhs", rhs_hbm, rhs)]
    pairs += [(("inv", e), inv_hbm.at[e], inv_stage.at[e]) for e in range(SLOTS)]
    pairs += [("lifts", lifts_hbm, lifts), ("coefs", coefs_hbm, coefs)]
    pairs += [(("blocks", e), blocks_hbm.at[e], stage.at[e]) for e in range(SLOTS)]
    pairs += [
        ("cblocks", cblocks_hbm, cblocks), ("cinv", cinv_hbm, cinv),
        ("clifts", clifts_hbm, clifts), ("ccoefs", ccoefs_hbm, ccoefs),
        ("lift", lift_hbm, lift_tab), ("restrict", restrict_hbm, restrict_tab),
        ("face", face_hbm, face_tab),
    ]
    for name, src, dst in pairs:
        loads[name] = pltpu.make_async_copy(src, dst, load_sem.at[count])
        loads[name].start()
        count += 1

    barrier = pltpu.get_barrier_semaphore()
    for has, device in sides:
        @pl.when(has)
        def _():
            pl.semaphore_signal(barrier, 1, device_id=device, device_id_type=MESH)

    for face in range(4):
        @pl.when(jnp.logical_not(sides[face][0]))
        def _():
            for r in range(3):
                f_recv[r, face] = jnp.zeros((NFACE, RHS), f32)
            for r in range(4):
                c_recv[r, face] = jnp.zeros((HALO, RHS), f32)
    for r in range(4):
        for face in range(4):
            c_send[r, face, pl.ds(16, 8), :] = jnp.zeros((8, RHS), f32)

    local, slot, cross = {}, {}, {}
    for e in range(SLOTS):
        for f in range(6):
            g = nbr[e, f]
            here = jnp.logical_and(g >= base, g < base + SLOTS)
            local[e, f] = jnp.where(here, 1, 0)
            slot[e, f] = jnp.clip(g - base, 0, SLOTS - 1)
            if f < 4:
                cross[e, f] = jnp.where(jnp.logical_and(g >= 0, jnp.logical_not(here)), 1, 0)
    owner = [
        jnp.clip(sum(e * cross[e, f] for e in range(1, SLOTS)), 0, SLOTS - 1) for f in range(4)
    ]
    weight = {key: value.astype(f32) for key, value in cross.items()}

    def transfer(send, recv, round_index, sem_row, face, target):
        return pltpu.make_async_remote_copy(
            src_ref=send.at[round_index, face],
            dst_ref=recv.at[round_index, target],
            send_sem=send_sem.at[sem_row, face],
            recv_sem=recv_sem.at[sem_row, target],
            device_id=sides[face][1],
            device_id_type=MESH,
        )

    def start_all(send, recv, round_index, sem_row):
        for face in range(4):
            @pl.when(sides[face][0])
            def _():
                transfer(send, recv, round_index, sem_row, face, face ^ 1).start()

    def wait_all(send, recv, round_index, sem_row):
        for face in range(4):
            @pl.when(sides[face][0])
            def _():
                transfer(send, recv, round_index, sem_row, face, face).wait_recv()

    def send_fine(round_index, sem_row):
        for face in range(4):
            f_send[round_index, face] = trace(v, owner[face], face)
        start_all(f_send, f_recv, round_index, sem_row)

    def send_coarse(round_index, sem_row):
        for face in range(4):
            coarse_trace_to(w, owner[face], face, c_send.at[round_index, face])
        start_all(c_send, c_recv, round_index, sem_row)

    loads["rhs"].wait()
    for e in range(SLOTS):
        live = jnp.where(e < counts[0], 1.0, 0.0)
        rhs[e] = rhs[e] * live
        loads["inv", e].wait()
        left_d[e] = pack_left(0.8 * inv_stage[e])
        v[e] = product(left_d[e], pack_right(rhs[e]))
    peers = 4 - sum(jnp.where(has, 0, 1) for has, device in sides)
    pl.semaphore_wait(barrier, peers)
    send_fine(0, 0)

    loads["lifts"].wait()
    loads["coefs"].wait()
    lift_high, lift_low = [], []
    for f in range(6):
        high, low = halves(lifts[f])
        lift_high.append(high)
        lift_low.append(low)
    gap = jnp.zeros((NF, 32), bf16)
    lift_h[...] = jnp.concatenate(lift_high + [gap], axis=1)
    lift_l[...] = jnp.concatenate(lift_low + [gap], axis=1)
    coef_sq[...] = jnp.zeros((128, 128), f32)
    for e in range(SLOTS):
        coef_sq[pl.ds(8 * e, 6), pl.ds(0, NFACE)] = coefs[e]
    columns = jnp.transpose(coef_sq[...])
    for e in range(SLOTS):
        for f in range(6):
            column = columns[:NFACE, 8 * e + f : 8 * e + f + 1] * local[e, f].astype(f32)
            coef_cols[e, f] = jnp.broadcast_to(column, (NFACE, RHS))
    x_h[pl.ds(480, 32), :] = jnp.zeros((32, SLOTS * RHS), bf16)
    x_l[pl.ds(480, 32), :] = jnp.zeros((32, SLOTS * RHS), bf16)
    for e in range(SLOTS):
        loads["blocks", e].wait()
        left_a[e] = pack_left(stage[e])

    def local_residual():
        for e in range(SLOTS):
            for f in range(6):
                high, low = halves(coef_cols[e, f] * trace(v, slot[e, f], f ^ 1))
                x_h[pl.ds(NFACE * f, NFACE), pl.ds(RHS * e, RHS)] = high
                x_l[pl.ds(NFACE * f, NFACE), pl.ds(RHS * e, RHS)] = low
        for pair in range(2):
            cols = pl.ds(256 * pair, 256)
            coupled = (
                jnp.dot(lift_h[...], x_h[:, cols], preferred_element_type=f32)
                + jnp.dot(lift_h[...], x_l[:, cols], preferred_element_type=f32)
                + jnp.dot(lift_l[...], x_h[:, cols], preferred_element_type=f32)
            )
            for half in range(2):
                e = 2 * pair + half
                block = product(left_a[e], pack_right(v[e]))
                r_loc[e] = rhs[e] - block - coupled[:, 128 * half : 128 * half + 128]

    def presweep():
        for e in range(SLOTS):
            vpre[e] = v[e] + product(left_d[e], pack_right(r_loc[e]))

    def cross_terms(left, recv, round_index):
        return [
            product(left[f], twice(recv[round_index, f], 128)) for f in range(4)
        ]

    def combine(terms, src, dst):
        for e in range(SLOTS):
            total = src[e]
            for f in range(4):
                total = total - weight[e, f] * terms[f]
            dst[e] = total

    local_residual()
    presweep()
    scaled = []
    for f in range(4):
        coef_row = coefs[owner[f], pl.ds(f, 1), :]
        scaled.append(pad_lanes(lifts[f] * coef_row, 128))
    rights = [pack_right(s) for s in scaled]
    for f in range(4):
        high, low = halves(product(left_d[owner[f]], rights[f]))
        cross_l[f] = jnp.concatenate([high, low], axis=1)

    wait_all(f_send, f_recv, 0, 0)
    combine(cross_terms(cross_l, f_recv, 0), vpre, v)
    send_fine(1, 1)

    local_residual()
    for name in ("cblocks", "cinv", "clifts", "ccoefs", "lift", "restrict", "face"):
        loads[name].wait()
    for e in range(SLOTS):
        left_ip[e] = pack_left(
            jnp.dot(0.2 * cinv[e], restrict_tab[...], precision=highest, preferred_element_type=f32)
        )
    for f in range(4):
        high, low = halves(product(left_ip[owner[f]], rights[f]))
        cross_k[f] = jnp.concatenate([high, low], axis=1)
    for e in range(SLOTS):
        w1[e] = product(left_ip[e], pack_right(r_loc[e]))
    t = lax.broadcasted_iota(jnp.int32, (128, 256), 0)
    lane = lax.broadcasted_iota(jnp.int32, (128, 256), 1)
    for e in range(SLOTS):
        def placed(matrix, target):
            high, low = halves(pad_lanes(matrix, 128))
            both = jnp.concatenate([high, low], axis=0)
            chosen = jnp.where(lane == target, 1.0, 0.0).astype(bf16)
            out = jnp.dot(both, chosen, preferred_element_type=f32)
            return out[:NC] + out[NC:]

        total = placed(cblocks[e], jnp.where(t < NC, t + NC * e, -1))
        for f in range(6):
            target = local[e, f] * (coarse_rows(f ^ 1, t) + NC * slot[e, f] + 1)
            if f < 4:
                target = target + cross[e, f] * (halo_rows(f, t) + 4 * NC + HALO * f + 1)
            target = jnp.where(t < NCF, target - 1, -1)
            total = total + placed(clifts[f] * ccoefs[e, pl.ds(f, 1), :], target)
        row = lax.broadcasted_iota(jnp.int32, (NC, 256), 0)
        col = lax.broadcasted_iota(jnp.int32, (NC, 256), 1)
        unit = jnp.where(col == row + NC * e, 1.0, 0.0)
        full = unit - jnp.dot(
            0.8 * cinv[e], total, precision=highest, preferred_element_type=f32
        )
        coarse_m[e] = full

    wait_all(f_send, f_recv, 1, 1)
    combine(cross_terms(cross_k, f_recv, 1), w1, w)
    for e in range(SLOTS):
        w1[e] = w[e]
    send_coarse(0, 2)

    left_high, left_low = halves(coarse_m[...].reshape(SLOTS * NC, 256))
    left_m = jnp.concatenate([left_high, left_low], axis=0)
    for f, term in enumerate(cross_terms(cross_l, f_recv, 1)):
        z_old[f] = term
    for f in range(4):
        high, low = halves(product(cross_l[f], face_tab[f]))
        cross_g[f] = jnp.concatenate([high, low], axis=1)

    for sweep in range(3):
        wait_all(c_send, c_recv, sweep, 2 + sweep)
        state = jnp.concatenate(
            [w[...].reshape(SLOTS * NC, RHS), c_recv[sweep].reshape(4 * HALO, RHS)], axis=0
        )
        high, low = halves(state)
        moved = jnp.dot(
            left_m, jnp.concatenate([high, low], axis=1), preferred_element_type=f32
        )
        moved = moved[: 4 * NC, :128] + (moved[: 4 * NC, 128:] + moved[4 * NC :, :128])
        w[...] = w1[...] + moved.reshape(SLOTS, NC, RHS)
        send_coarse(sweep + 1, 3 + sweep)

    for e in range(SLOTS):
        v[e] = v[e] + product(lift_tab[...], twice(w[e], 64))
    local_residual()
    presweep()
    combine([z_old[f] for f in range(4)], vpre, vpre)
    wait_all(c_send, c_recv, 3, 5)
    combine(cross_terms(cross_g, c_recv, 3), vpre, v)
    send_fine(2, 6)
    local_residual()
    presweep()
    wait_all(f_send, f_recv, 2, 6)
    combine(cross_terms(cross_l, f_recv, 2), vpre, out)

    for face in range(4):
        @pl.when(sides[face][0])
        def _():
            for r, row in ((0, 0), (1, 1), (2, 6)):
                transfer(f_send, f_recv, r, row, face, face ^ 1).wait_send()
            for r in range(4):
                transfer(c_send, c_recv, r, 2 + r, face, face ^ 1).wait_send()


def body(*args):
    any_spec = pl.BlockSpec(memory_space=pl.ANY)
    smem_spec = pl.BlockSpec(memory_space=pltpu.SMEM)
    constants = [jnp.asarray(c) for c in tables()]
    vm = pltpu.VMEM
    scratch = [
        vm((SLOTS, NF, RHS), f32), vm((SLOTS, NF, NF), f32), vm((SLOTS, NF, NF), f32),
        vm((6, NF, NFACE), f32), vm((SLOTS, 6, NFACE), f32),
        vm((SLOTS, NC, NC), f32), vm((SLOTS, NC, NC), f32), vm((6, NC, NCF), f32),
        vm((SLOTS, 6, NCF), f32),
        vm((NF, 128), bf16), vm((NC, NF), f32), vm((4, 256, 256), bf16),
        vm((SLOTS, NF, 640), bf16), vm((SLOTS, NF, 640), bf16),
        vm((NF, 512), bf16), vm((NF, 512), bf16),
        vm((SLOTS, 6, NFACE, RHS), f32), vm((128, 128), f32),
        vm((SLOTS, NF, RHS), f32), vm((SLOTS, NF, RHS), f32),
        vm((512, 512), bf16), vm((512, 512), bf16), vm((SLOTS, NF, RHS), f32),
        vm((4, NF, 256), bf16), vm((4, NF, 256), bf16), vm((4, NC, 256), bf16),
        vm((SLOTS, NC, 640), bf16), vm((SLOTS, NC, 256), f32),
        vm((SLOTS, NC, RHS), f32), vm((SLOTS, NC, RHS), f32),
        vm((4, NF, RHS), f32),
        vm((3, 4, NFACE, RHS), f32), vm((3, 4, NFACE, RHS), f32),
        vm((4, 4, HALO, RHS), f32), vm((4, 4, HALO, RHS), f32),
        pltpu.SemaphoreType.DMA((24,)),
        pltpu.SemaphoreType.DMA((7, 4)), pltpu.SemaphoreType.DMA((7, 4)),
    ]
    return pl.pallas_call(
        kernel,
        out_shape=jax.ShapeDtypeStruct((SLOTS, NF, RHS), f32),
        in_specs=[any_spec] * 9 + [smem_spec] * 2 + [any_spec] * 3,
        out_specs=pl.BlockSpec(memory_space=pltpu.VMEM),
        scratch_shapes=scratch,
        compiler_params=pltpu.CompilerParams(collective_id=0, has_side_effects=True),
        name="cycle",
    )(*args, *constants)


def solution(mesh):
    split = ("wide", "narrow")
    placed = (
        P(split, None, None),
        P(split, None, None),
        P(split, None, None),
        P(),
        P(split, None, None),
        P(split, None, None),
        P(split, None, None),
        P(),
        P(split, None, None),
        P(split, None),
        P(split),
    )
    return jax.shard_map(
        body, mesh=mesh, in_specs=placed, out_specs=P(split, None, None), check_vma=False
    )
```

```python
import jax
import jax.numpy as jnp
import numpy as np
from jax import lax
from jax.experimental import pallas as pl
from jax.experimental.pallas import tpu as pltpu
from jax.sharding import PartitionSpec as P

NVAR = 5
SLOTS = 4
NF = 320
NFACE = 80
NC = 40
NCF = 20
HALO = 24
RHS = 128
WIDE = 8
NARROW = 32
MESH = pl.DeviceIdType.MESH
highest = lax.Precision.HIGHEST
bf16 = jnp.bfloat16
f32 = jnp.float32


def linear_table():
    points = np.array([-1.0, -1.0 / np.sqrt(5.0), 1.0 / np.sqrt(5.0), 1.0])
    return np.stack([(1.0 - points) / 2.0, (1.0 + points) / 2.0], axis=1)


def split_np(values):
    values = values.astype(np.float32)
    high = values.astype(bf16)
    low = (values - high.astype(np.float32)).astype(bf16)
    return high, low


def tables():
    linear = linear_table()
    cube = np.kron(np.kron(linear, linear), linear)
    prolong = np.kron(np.eye(NVAR), cube).astype(np.float32)
    flat = np.kron(np.eye(NVAR), np.kron(linear, linear)).astype(np.float32)
    high, low = split_np(prolong)
    lift = np.zeros((NF, 128), high.dtype)
    lift[:, :NC] = high
    lift[:, 64 : 64 + NC] = low
    wide_order = np.zeros((4, NFACE, HALO), np.float32)
    for face in range(4):
        for t in range(NCF):
            position = (t % 4) * 5 + t // 4 if face < 2 else (t % 2) * 10 + t // 2
            wide_order[face, :, position] = flat[:, t]
    face_tab = np.zeros((4, 256, 256), high.dtype)
    for face in range(4):
        high, low = split_np(wide_order[face])
        for start in (0, 128):
            face_tab[face, start : start + NFACE, :HALO] = high
            face_tab[face, start : start + NFACE, 128 : 128 + HALO] = low
    return lift, np.ascontiguousarray(prolong.T), face_tab


def halves(x):
    high = x.astype(bf16)
    low = (x - high.astype(f32)).astype(bf16)
    return high, low


def pack_left(x):
    high, low = halves(x)
    return jnp.concatenate(
        [high[:, :256], low[:, :256], jnp.concatenate([high[:, 256:], low[:, 256:]], axis=1)],
        axis=1,
    )


def pack_right(x):
    high, low = halves(x)
    both = jnp.concatenate([high, low], axis=1)
    main, rest = both[:256], both[256:]
    return jnp.concatenate([main, main, rest, rest], axis=0)


def product(left, right):
    out = jnp.dot(left, right, preferred_element_type=f32)
    return out[:, :128] + out[:, 128:]


def pad_rows(x, rows):
    return jnp.concatenate([x, jnp.zeros((rows - x.shape[0], x.shape[1]), x.dtype)], axis=0)


def pad_lanes(x, lanes):
    return jnp.concatenate([x, jnp.zeros((x.shape[0], lanes - x.shape[1]), x.dtype)], axis=1)


def twice(x, rows):
    high, low = halves(pad_rows(x, rows))
    both = jnp.concatenate([high, low], axis=1)
    return jnp.concatenate([both, both], axis=0)


def trace(ref, slot, face):
    odd = face & 1
    if face < 2:
        return jnp.concatenate(
            [ref[slot, pl.ds(64 * v + 48 * odd, 16), :] for v in range(NVAR)], axis=0
        )
    if face < 4:
        tiles = ref[slot].reshape(20, 16, RHS)[:, 8 * odd : 8 * odd + 8]
        pairs = tiles.reshape(10, 2, 8, RHS)
        first, second = pairs[:, 0], pairs[:, 1]
        upper = lax.broadcasted_iota(jnp.int32, (10, 8, RHS), 1) < 4
        if odd:
            out = jnp.where(upper, pltpu.roll(first, 4, 1), second)
        else:
            out = jnp.where(upper, first, pltpu.roll(second, 4, 1))
        return out.reshape(NFACE, RHS)
    return ref[slot, pl.ds(3 * odd, NFACE, stride=4), :]


def coarse_trace_to(ref, slot, face, out):
    odd = face & 1
    if face < 2:
        for q in range(4):
            out[pl.ds(5 * q, 5), :] = ref[slot, pl.ds(4 * odd + q, 5, stride=8), :]
    else:
        for q in range(2):
            out[pl.ds(10 * q, 10), :] = ref[slot, pl.ds(2 * odd + q, 10, stride=4), :]


def coarse_rows(face, t):
    odd = face & 1
    var = lax.shift_right_logical(t, 2)
    a = lax.shift_right_logical(t, 1) & 1
    b = t & 1
    if face < 2:
        return var * 8 + 4 * odd + a * 2 + b
    if face < 4:
        return var * 8 + a * 4 + 2 * odd + b
    return var * 8 + a * 4 + b * 2 + odd


def halo_rows(face, t):
    if face < 2:
        return (t & 3) * 5 + lax.shift_right_logical(t, 2)
    return (t & 1) * 10 + lax.shift_right_logical(t, 1)


def kernel(
    rhs_hbm, blocks_hbm, inv_hbm, lifts_hbm, coefs_hbm,
    cblocks_hbm, cinv_hbm, clifts_hbm, ccoefs_hbm, nbr_hbm, counts,
    lift_hbm, restrict_hbm, face_hbm,
    out,
    rhs, stage, inv_stage, lifts, coefs, cblocks, cinv, clifts, ccoefs, lift_tab, restrict_tab, face_tab,
    left_a, left_d, lift_h, lift_l, coef_cols, coef_sq,
    v, vpre, x_h, x_l, r_loc, cross_l, cross_g, cross_k, left_ip, coarse_m, w1, w,
    z_old, f_send, f_recv, c_send, c_recv,
    nbr, load_sem, send_sem, recv_sem,
):
    wide = lax.axis_index("wide")
    narrow = lax.axis_index("narrow")
    base = (wide * NARROW + narrow) * SLOTS
    sides = [
        (wide > 0, {"wide": wide - 1}),
        (wide < WIDE - 1, {"wide": wide + 1}),
        (narrow > 0, {"narrow": narrow - 1}),
        (narrow < NARROW - 1, {"narrow": narrow + 1}),
    ]

    loads = {}
    count = 0
    pairs = [("nbr", nbr_hbm, nbr), ("rhs", rhs_hbm, rhs)]
    pairs += [(("inv", e), inv_hbm.at[e], inv_stage.at[e]) for e in range(SLOTS)]
    pairs += [("lifts", lifts_hbm, lifts), ("coefs", coefs_hbm, coefs)]
    pairs += [(("blocks", e), blocks_hbm.at[e], stage.at[e]) for e in range(SLOTS)]
    pairs += [
        ("cblocks", cblocks_hbm, cblocks), ("cinv", cinv_hbm, cinv),
        ("clifts", clifts_hbm, clifts), ("ccoefs", ccoefs_hbm, ccoefs),
        ("lift", lift_hbm, lift_tab), ("restrict", restrict_hbm, restrict_tab),
        ("face", face_hbm, face_tab),
    ]
    for name, src, dst in pairs:
        loads[name] = pltpu.make_async_copy(src, dst, load_sem.at[count])
        loads[name].start()
        count += 1

    barrier = pltpu.get_barrier_semaphore()
    for has, device in sides:
        @pl.when(has)
        def _():
            pl.semaphore_signal(barrier, 1, device_id=device, device_id_type=MESH)

    for face in range(4):
        @pl.when(jnp.logical_not(sides[face][0]))
        def _():
            for r in range(3):
                f_recv[r, face] = jnp.zeros((NFACE, RHS), f32)
            for r in range(4):
                c_recv[r, face] = jnp.zeros((HALO, RHS), f32)
    for r in range(4):
        for face in range(4):
            c_send[r, face, pl.ds(16, 8), :] = jnp.zeros((8, RHS), f32)

    loads["nbr"].wait()
    local, slot, cross = {}, {}, {}
    for e in range(SLOTS):
        for f in range(6):
            g = nbr[e, f]
            here = jnp.logical_and(g >= base, g < base + SLOTS)
            local[e, f] = jnp.where(here, 1, 0)
            slot[e, f] = jnp.clip(g - base, 0, SLOTS - 1)
            if f < 4:
                cross[e, f] = jnp.where(jnp.logical_and(g >= 0, jnp.logical_not(here)), 1, 0)
    owner = [
        jnp.clip(sum(e * cross[e, f] for e in range(1, SLOTS)), 0, SLOTS - 1) for f in range(4)
    ]
    weight = {key: value.astype(f32) for key, value in cross.items()}

    def transfer(send, recv, round_index, sem_row, face, target):
        return pltpu.make_async_remote_copy(
            src_ref=send.at[round_index, face],
            dst_ref=recv.at[round_index, target],
            send_sem=send_sem.at[sem_row, face],
            recv_sem=recv_sem.at[sem_row, target],
            device_id=sides[face][1],
            device_id_type=MESH,
        )

    def start_all(send, recv, round_index, sem_row):
        for face in range(4):
            @pl.when(sides[face][0])
            def _():
                transfer(send, recv, round_index, sem_row, face, face ^ 1).start()

    def wait_all(send, recv, round_index, sem_row):
        for face in range(4):
            @pl.when(sides[face][0])
            def _():
                transfer(send, recv, round_index, sem_row, face, face).wait_recv()

    def send_fine(round_index, sem_row):
        for face in range(4):
            f_send[round_index, face] = trace(v, owner[face], face)
        start_all(f_send, f_recv, round_index, sem_row)

    def send_coarse(round_index, sem_row):
        for face in range(4):
            coarse_trace_to(w, owner[face], face, c_send.at[round_index, face])
        start_all(c_send, c_recv, round_index, sem_row)

    loads["rhs"].wait()
    for e in range(SLOTS):
        live = jnp.where(e < counts[0], 1.0, 0.0)
        rhs[e] = rhs[e] * live
        loads["inv", e].wait()
        left_d[e] = pack_left(0.8 * inv_stage[e])
        v[e] = product(left_d[e], pack_right(rhs[e]))
    peers = 4 - sum(jnp.where(has, 0, 1) for has, device in sides)
    pl.semaphore_wait(barrier, peers)
    send_fine(0, 0)

    loads["lifts"].wait()
    loads["coefs"].wait()
    flat = pad_rows(jnp.concatenate([lifts[f] for f in range(6)], axis=0), 512)
    upright = jnp.transpose(pad_lanes(flat, 384))[:NF]
    lift_high, lift_low = halves(upright)
    lift_h[...] = lift_high
    lift_l[...] = lift_low
    coef_sq[...] = jnp.zeros((128, 128), f32)
    for f in range(6):
        coef_sq[pl.ds(8 * f, SLOTS), pl.ds(0, NFACE)] = coefs[f]
    columns = jnp.transpose(coef_sq[...])
    for e in range(SLOTS):
        for f in range(6):
            column = columns[:NFACE, 8 * f + e : 8 * f + e + 1] * local[e, f].astype(f32)
            coef_cols[e, f] = jnp.broadcast_to(column, (NFACE, RHS))
    x_h[pl.ds(480, 32), :] = jnp.zeros((32, SLOTS * RHS), bf16)
    x_l[pl.ds(480, 32), :] = jnp.zeros((32, SLOTS * RHS), bf16)
    for e in range(SLOTS):
        loads["blocks", e].wait()
        left_a[e] = pack_left(stage[e])

    def local_residual():
        for e in range(SLOTS):
            for f in range(6):
                high, low = halves(coef_cols[e, f] * trace(v, slot[e, f], f ^ 1))
                x_h[pl.ds(NFACE * f, NFACE), pl.ds(RHS * e, RHS)] = high
                x_l[pl.ds(NFACE * f, NFACE), pl.ds(RHS * e, RHS)] = low
        for pair in range(2):
            cols = pl.ds(256 * pair, 256)
            coupled = (
                jnp.dot(lift_h[...], x_h[:, cols], preferred_element_type=f32)
                + jnp.dot(lift_h[...], x_l[:, cols], preferred_element_type=f32)
                + jnp.dot(lift_l[...], x_h[:, cols], preferred_element_type=f32)
            )
            for half in range(2):
                e = 2 * pair + half
                block = product(left_a[e], pack_right(v[e]))
                r_loc[e] = rhs[e] - block - coupled[:, 128 * half : 128 * half + 128]

    def presweep():
        for e in range(SLOTS):
            vpre[e] = v[e] + product(left_d[e], pack_right(r_loc[e]))

    def cross_terms(left, recv, round_index):
        return [
            product(left[f], twice(recv[round_index, f], 128)) for f in range(4)
        ]

    def combine(terms, src, dst):
        for e in range(SLOTS):
            total = src[e]
            for f in range(4):
                total = total - weight[e, f] * terms[f]
            dst[e] = total

    local_residual()
    presweep()
    scaled = []
    for f in range(4):
        coef_row = sum(weight[e, f] * coefs[f, pl.ds(e, 1), :] for e in range(SLOTS))
        square = jnp.transpose(pad_lanes(pad_rows(lifts[f], 128), 384))[:NF]
        scaled.append(square * pad_lanes(coef_row, 128))
    rights = [pack_right(s) for s in scaled]
    for f in range(4):
        high, low = halves(product(left_d[owner[f]], rights[f]))
        cross_l[f] = jnp.concatenate([high, low], axis=1)

    wait_all(f_send, f_recv, 0, 0)
    combine(cross_terms(cross_l, f_recv, 0), vpre, v)
    send_fine(1, 1)

    local_residual()
    for name in ("cblocks", "cinv", "clifts", "ccoefs", "lift", "restrict", "face"):
        loads[name].wait()
    for e in range(SLOTS):
        left_ip[e] = pack_left(
            jnp.dot(0.2 * cinv[e], restrict_tab[...], precision=highest, preferred_element_type=f32)
        )
    for f in range(4):
        high, low = halves(product(left_ip[owner[f]], rights[f]))
        cross_k[f] = jnp.concatenate([high, low], axis=1)
    for e in range(SLOTS):
        w1[e] = product(left_ip[e], pack_right(r_loc[e]))
    clift_sq = [
        jnp.transpose(pad_lanes(pad_rows(clifts[f], 128), 128))[:NC] for f in range(6)
    ]
    t = lax.broadcasted_iota(jnp.int32, (128, 256), 0)
    lane = lax.broadcasted_iota(jnp.int32, (128, 256), 1)
    for e in range(SLOTS):
        def placed(matrix, target):
            high, low = halves(matrix)
            both = jnp.concatenate([high, low], axis=0)
            chosen = jnp.where(lane == target, 1.0, 0.0).astype(bf16)
            out = jnp.dot(both, chosen, preferred_element_type=f32)
            return out[:NC] + out[NC:]

        total = placed(pad_lanes(cblocks[e], 128), jnp.where(t < NC, t + NC * e, -1))
        for f in range(6):
            target = local[e, f] * (coarse_rows(f ^ 1, t) + NC * slot[e, f] + 1)
            if f < 4:
                target = target + cross[e, f] * (halo_rows(f, t) + 4 * NC + HALO * f + 1)
            target = jnp.where(t < NCF, target - 1, -1)
            total = total + placed(clift_sq[f] * pad_lanes(ccoefs[f, pl.ds(e, 1), :], 128), target)
        row = lax.broadcasted_iota(jnp.int32, (NC, 256), 0)
        col = lax.broadcasted_iota(jnp.int32, (NC, 256), 1)
        unit = jnp.where(col == row + NC * e, 1.0, 0.0)
        full = unit - jnp.dot(
            0.8 * cinv[e], total, precision=highest, preferred_element_type=f32
        )
        coarse_m[e] = full

    wait_all(f_send, f_recv, 1, 1)
    combine(cross_terms(cross_k, f_recv, 1), w1, w)
    for e in range(SLOTS):
        w1[e] = w[e]
    send_coarse(0, 2)

    left_high, left_low = halves(coarse_m[...].reshape(SLOTS * NC, 256))
    left_m = jnp.concatenate([left_high, left_low], axis=0)
    for f, term in enumerate(cross_terms(cross_l, f_recv, 1)):
        z_old[f] = term
    for f in range(4):
        high, low = halves(product(cross_l[f], face_tab[f]))
        cross_g[f] = jnp.concatenate([high, low], axis=1)

    for sweep in range(3):
        wait_all(c_send, c_recv, sweep, 2 + sweep)
        state = jnp.concatenate(
            [w[...].reshape(SLOTS * NC, RHS), c_recv[sweep].reshape(4 * HALO, RHS)], axis=0
        )
        high, low = halves(state)
        moved = jnp.dot(
            left_m, jnp.concatenate([high, low], axis=1), preferred_element_type=f32
        )
        moved = moved[: 4 * NC, :128] + (moved[: 4 * NC, 128:] + moved[4 * NC :, :128])
        w[...] = w1[...] + moved.reshape(SLOTS, NC, RHS)
        send_coarse(sweep + 1, 3 + sweep)

    for e in range(SLOTS):
        v[e] = v[e] + product(lift_tab[...], twice(w[e], 64))
    local_residual()
    presweep()
    combine([z_old[f] for f in range(4)], vpre, vpre)
    wait_all(c_send, c_recv, 3, 5)
    combine(cross_terms(cross_g, c_recv, 3), vpre, v)
    send_fine(2, 6)
    local_residual()
    presweep()
    wait_all(f_send, f_recv, 2, 6)
    combine(cross_terms(cross_l, f_recv, 2), vpre, out)

    for face in range(4):
        @pl.when(sides[face][0])
        def _():
            for r, row in ((0, 0), (1, 1), (2, 6)):
                transfer(f_send, f_recv, r, row, face, face ^ 1).wait_send()
            for r in range(4):
                transfer(c_send, c_recv, r, 2 + r, face, face ^ 1).wait_send()


def body(*args):
    args = list(args)
    for i in (3, 7):
        args[i] = jnp.transpose(args[i], (0, 2, 1))
    for i in (4, 8):
        args[i] = jnp.transpose(args[i], (1, 0, 2))
    any_spec = pl.BlockSpec(memory_space=pltpu.HBM)
    constants = [jnp.asarray(c) for c in tables()]
    pin = lambda x: pltpu.with_memory_space_constraint(x, pltpu.HBM)
    args = [pin(a) for a in args[:10]] + args[10:]
    constants = [pin(c) for c in constants]
    vm = pltpu.VMEM
    scratch = [
        vm((SLOTS, NF, RHS), f32), vm((SLOTS, NF, NF), f32), vm((SLOTS, NF, NF), f32),
        vm((6, NFACE, NF), f32), vm((6, SLOTS, NFACE), f32),
        vm((SLOTS, NC, NC), f32), vm((SLOTS, NC, NC), f32), vm((6, NCF, NC), f32),
        vm((6, SLOTS, NCF), f32),
        vm((NF, 128), bf16), vm((NC, NF), f32), vm((4, 256, 256), bf16),
        vm((SLOTS, NF, 640), bf16), vm((SLOTS, NF, 640), bf16),
        vm((NF, 512), bf16), vm((NF, 512), bf16),
        vm((SLOTS, 6, NFACE, RHS), f32), vm((128, 128), f32),
        vm((SLOTS, NF, RHS), f32), vm((SLOTS, NF, RHS), f32),
        vm((512, 512), bf16), vm((512, 512), bf16), vm((SLOTS, NF, RHS), f32),
        vm((4, NF, 256), bf16), vm((4, NF, 256), bf16), vm((4, NC, 256), bf16),
        vm((SLOTS, NC, 640), bf16), vm((SLOTS, NC, 256), f32),
        vm((SLOTS, NC, RHS), f32), vm((SLOTS, NC, RHS), f32),
        vm((4, NF, RHS), f32),
        vm((3, 4, NFACE, RHS), f32), vm((3, 4, NFACE, RHS), f32),
        vm((4, 4, HALO, RHS), f32), vm((4, 4, HALO, RHS), f32),
        pltpu.SMEM((SLOTS, 6), jnp.int32),
        pltpu.SemaphoreType.DMA((24,)),
        pltpu.SemaphoreType.DMA((7, 4)), pltpu.SemaphoreType.DMA((7, 4)),
    ]
    return pl.pallas_call(
        kernel,
        out_shape=jax.ShapeDtypeStruct((SLOTS, NF, RHS), f32),
        in_specs=[any_spec] * 10 + [pl.BlockSpec(memory_space=pltpu.SMEM)] + [any_spec] * 3,
        out_specs=pl.BlockSpec(memory_space=pltpu.VMEM),
        scratch_shapes=scratch,
        compiler_params=pltpu.CompilerParams(collective_id=0, has_side_effects=True, vmem_limit_bytes=32 << 20),
        name="cycle",
    )(*args, *constants)


def solution(mesh):
    split = ("wide", "narrow")
    placed = (
        P(split, None, None),
        P(split, None, None),
        P(split, None, None),
        P(),
        P(split, None, None),
        P(split, None, None),
        P(split, None, None),
        P(),
        P(split, None, None),
        P(split, None),
        P(split),
    )
    return jax.shard_map(
        body, mesh=mesh, in_specs=placed, out_specs=P(split, None, None), check_vma=False
    )
```

```python
import jax
import jax.numpy as jnp
import numpy as np
from jax import lax
from jax.experimental import pallas as pl
from jax.experimental.pallas import tpu as pltpu
from jax.sharding import PartitionSpec as P

NVAR = 5
SLOTS = 4
NF = 320
NFACE = 80
NC = 40
NCF = 20
HALO = 24
RHS = 128
WIDE = 8
NARROW = 32
MESH = pl.DeviceIdType.MESH
highest = lax.Precision.HIGHEST
STEPS = [(-1, 0), (1, 0), (0, -1), (0, 1)]
REACH = STEPS + [(-2, 0), (2, 0), (0, -2), (0, 2), (-1, -1), (-1, 1), (1, -1), (1, 1)]
bf16 = jnp.bfloat16
f32 = jnp.float32


def offset(face, other):
    return tuple(a + b for a, b in zip(STEPS[face], STEPS[other]))


def linear_table():
    points = np.array([-1.0, -1.0 / np.sqrt(5.0), 1.0 / np.sqrt(5.0), 1.0])
    return np.stack([(1.0 - points) / 2.0, (1.0 + points) / 2.0], axis=1)


def split_np(values):
    values = values.astype(np.float32)
    high = values.astype(bf16)
    low = (values - high.astype(np.float32)).astype(bf16)
    return high, low


def tables():
    linear = linear_table()
    cube = np.kron(np.kron(linear, linear), linear)
    prolong = np.kron(np.eye(NVAR), cube).astype(np.float32)
    flat = np.kron(np.eye(NVAR), np.kron(linear, linear)).astype(np.float32)
    high, low = split_np(prolong)
    lift = np.zeros((NF, 128), high.dtype)
    lift[:, :NC] = high
    lift[:, 64 : 64 + NC] = low
    wide_order = np.zeros((4, NFACE, HALO), np.float32)
    for face in range(4):
        for t in range(NCF):
            position = (t % 4) * 5 + t // 4 if face < 2 else (t % 2) * 10 + t // 2
            wide_order[face, :, position] = flat[:, t]
    face_tab = np.zeros((4, 256, 256), high.dtype)
    for face in range(4):
        high, low = split_np(wide_order[face])
        for start in (0, 128):
            face_tab[face, start : start + NFACE, :HALO] = high
            face_tab[face, start : start + NFACE, 128 : 128 + HALO] = low
    return lift, np.ascontiguousarray(prolong.T), face_tab


def halves(x):
    high = x.astype(bf16)
    low = (x - high.astype(f32)).astype(bf16)
    return high, low


def pack_left(x):
    high, low = halves(x)
    return jnp.concatenate(
        [high[:, :256], low[:, :256], jnp.concatenate([high[:, 256:], low[:, 256:]], axis=1)],
        axis=1,
    )


def pack_right(x):
    high, low = halves(x)
    both = jnp.concatenate([high, low], axis=1)
    main, rest = both[:256], both[256:]
    return jnp.concatenate([main, main, rest, rest], axis=0)


def product(left, right):
    out = jnp.dot(left, right, preferred_element_type=f32)
    return out[:, :128] + out[:, 128:]


def pad_rows(x, rows):
    return jnp.concatenate([x, jnp.zeros((rows - x.shape[0], x.shape[1]), x.dtype)], axis=0)


def pad_lanes(x, lanes):
    return jnp.concatenate([x, jnp.zeros((x.shape[0], lanes - x.shape[1]), x.dtype)], axis=1)


def twice(x, rows):
    high, low = halves(pad_rows(x, rows))
    both = jnp.concatenate([high, low], axis=1)
    return jnp.concatenate([both, both], axis=0)


def trace(ref, slot, face):
    odd = face & 1
    if face < 2:
        return jnp.concatenate(
            [ref[slot, pl.ds(64 * v + 48 * odd, 16), :] for v in range(NVAR)], axis=0
        )
    if face < 4:
        tiles = ref[slot].reshape(20, 16, RHS)[:, 8 * odd : 8 * odd + 8]
        pairs = tiles.reshape(10, 2, 8, RHS)
        first, second = pairs[:, 0], pairs[:, 1]
        upper = lax.broadcasted_iota(jnp.int32, (10, 8, RHS), 1) < 4
        if odd:
            out = jnp.where(upper, pltpu.roll(first, 4, 1), second)
        else:
            out = jnp.where(upper, first, pltpu.roll(second, 4, 1))
        return out.reshape(NFACE, RHS)
    return ref[slot, pl.ds(3 * odd, NFACE, stride=4), :]


def coarse_trace_to(ref, slot, face, out):
    odd = face & 1
    if face < 2:
        for q in range(4):
            out[pl.ds(5 * q, 5), :] = ref[slot, pl.ds(4 * odd + q, 5, stride=8), :]
    else:
        for q in range(2):
            out[pl.ds(10 * q, 10), :] = ref[slot, pl.ds(2 * odd + q, 10, stride=4), :]


def coarse_rows(face, t):
    odd = face & 1
    var = lax.shift_right_logical(t, 2)
    a = lax.shift_right_logical(t, 1) & 1
    b = t & 1
    if face < 2:
        return var * 8 + 4 * odd + a * 2 + b
    if face < 4:
        return var * 8 + a * 4 + 2 * odd + b
    return var * 8 + a * 4 + b * 2 + odd


def halo_rows(face, t):
    if face < 2:
        return (t & 3) * 5 + lax.shift_right_logical(t, 2)
    return (t & 1) * 10 + lax.shift_right_logical(t, 1)


def kernel(
    rhs_hbm, blocks_hbm, inv_hbm, lifts_hbm, coefs_hbm,
    cblocks_hbm, cinv_hbm, clifts_hbm, ccoefs_hbm, nbr_hbm, counts,
    lift_hbm, restrict_hbm, face_hbm,
    out,
    rhs, stage, inv_stage, lifts, coefs, cblocks, cinv, clifts, ccoefs, lift_tab, restrict_tab, face_tab,
    left_a, left_d, lift_h, lift_l, coef_cols, coef_sq,
    v, vpre, x_h, x_l, r_loc, cross_l, cross_g, cross_k, left_ip, coarse_m, w1, w,
    z_old, f_send, f_recv, c_send, c_recv, far_recv, p_send, p_recv, o_send, o_recv, coarse_h, pre,
    nbr, load_sem, send_sem, recv_sem, far_send_sem, far_recv_sem,
):
    wide = lax.axis_index("wide")
    narrow = lax.axis_index("narrow")
    base = (wide * NARROW + narrow) * SLOTS

    def inside(dw, dn):
        conditions = []
        if dw < 0:
            conditions.append(wide >= -dw)
        if dw > 0:
            conditions.append(wide < WIDE - dw)
        if dn < 0:
            conditions.append(narrow >= -dn)
        if dn > 0:
            conditions.append(narrow < NARROW - dn)
        result = conditions[0]
        for condition in conditions[1:]:
            result = jnp.logical_and(result, condition)
        return result

    def place(dw, dn):
        return (wide + dw, narrow + dn)

    sides = [(inside(*STEPS[face]), place(*STEPS[face])) for face in range(4)]

    barrier = pltpu.get_barrier_semaphore()
    peers = 0
    for dw, dn in REACH:
        has = inside(dw, dn)
        peers = peers + jnp.where(has, 1, 0)

        @pl.when(has)
        def _():
            pl.semaphore_signal(barrier, 1, device_id=place(dw, dn), device_id_type=MESH)

    loads = {}
    count = 0
    pairs = [("nbr", nbr_hbm, nbr)]
    pairs += [(("rhs", e), rhs_hbm.at[e], rhs.at[e]) for e in range(SLOTS)]
    pairs += [(("inv", e), inv_hbm.at[e], inv_stage.at[e]) for e in range(SLOTS)]
    pairs += [("lifts", lifts_hbm, lifts), ("coefs", coefs_hbm, coefs)]
    pairs += [(("blocks", e), blocks_hbm.at[e], stage.at[e]) for e in range(SLOTS)]
    pairs += [
        ("cblocks", cblocks_hbm, cblocks), ("cinv", cinv_hbm, cinv),
        ("clifts", clifts_hbm, clifts), ("ccoefs", ccoefs_hbm, ccoefs),
        ("lift", lift_hbm, lift_tab), ("restrict", restrict_hbm, restrict_tab),
        ("face", face_hbm, face_tab),
    ]
    for name, src, dst in pairs:
        loads[name] = pltpu.make_async_copy(src, dst, load_sem.at[count])
        count += 1
    early = ["nbr"]
    for e in range(SLOTS):
        early += [("rhs", e), ("inv", e)]
    late = [name for name in loads if name not in early]
    for name in early:
        loads[name].start()

    for face in range(4):
        @pl.when(jnp.logical_not(sides[face][0]))
        def _():
            for r in range(3):
                f_recv[r, face] = jnp.zeros((NFACE, RHS), f32)
            for r in range(2):
                c_recv[r, face] = jnp.zeros((HALO, RHS), f32)
                p_recv[r, face] = jnp.zeros((HALO, RHS), f32)
            o_recv[face] = jnp.zeros((HALO, RHS), f32)
    tail = jnp.zeros((8, RHS), f32)
    for face in range(4):
        for r in range(2):
            c_send[r, face, pl.ds(16, 8), :] = tail
            p_send[r, face, pl.ds(16, 8), :] = tail
            far_recv[r, face, pl.ds(4 * HALO, 32), :] = jnp.zeros((32, RHS), f32)
        o_send[face, pl.ds(16, 8), :] = tail
        for other in range(4):
            if other != face ^ 1:
                @pl.when(jnp.logical_not(inside(*offset(face, other))))
                def _():
                    for r in range(2):
                        far_recv[r, face, pl.ds(HALO * other, HALO), :] = jnp.zeros((HALO, RHS), f32)

    loads["nbr"].wait()
    local, slot, cross = {}, {}, {}
    for e in range(SLOTS):
        for f in range(6):
            g = nbr[e, f]
            here = jnp.logical_and(g >= base, g < base + SLOTS)
            local[e, f] = jnp.where(here, 1, 0)
            slot[e, f] = jnp.clip(g - base, 0, SLOTS - 1)
            if f < 4:
                cross[e, f] = jnp.where(jnp.logical_and(g >= 0, jnp.logical_not(here)), 1, 0)
    owner = [
        jnp.clip(sum(e * cross[e, f] for e in range(1, SLOTS)), 0, SLOTS - 1) for f in range(4)
    ]
    weight = {key: value.astype(f32) for key, value in cross.items()}

    def transfer(send, recv, round_index, sem_row, face, target):
        return pltpu.make_async_remote_copy(
            src_ref=send.at[round_index, face],
            dst_ref=recv.at[round_index, target],
            send_sem=send_sem.at[sem_row, face],
            recv_sem=recv_sem.at[sem_row, target],
            device_id=sides[face][1],
            device_id_type=MESH,
        )

    def start_all(send, recv, round_index, sem_row):
        for face in range(4):
            @pl.when(sides[face][0])
            def _():
                transfer(send, recv, round_index, sem_row, face, face ^ 1).start()

    def wait_all(send, recv, round_index, sem_row):
        for face in range(4):
            @pl.when(sides[face][0])
            def _():
                transfer(send, recv, round_index, sem_row, face, face).wait_recv()

    def op_copy(face, target):
        return pltpu.make_async_remote_copy(
            src_ref=o_send.at[face],
            dst_ref=o_recv.at[target],
            send_sem=send_sem.at[7, face],
            recv_sem=recv_sem.at[7, target],
            device_id=sides[face][1],
            device_id_type=MESH,
        )

    def send_fine(round_index, sem_row):
        for face in range(4):
            f_send[round_index, face] = trace(v, owner[face], face)
        start_all(f_send, f_recv, round_index, sem_row)

    def far_copy(round_index, face, other, device):
        return pltpu.make_async_remote_copy(
            src_ref=c_send.at[round_index, face],
            dst_ref=far_recv.at[round_index, other ^ 1, pl.ds(HALO * (face ^ 1), HALO)],
            send_sem=far_send_sem.at[round_index, face, other],
            recv_sem=far_recv_sem.at[round_index, other ^ 1, face ^ 1],
            device_id=device,
            device_id_type=MESH,
        )

    def far_each(act):
        for face in range(4):
            for other in range(4):
                if other != face ^ 1:
                    @pl.when(inside(*offset(face, other)))
                    def _():
                        act(face, other, place(*offset(face, other)))

    def far_start(round_index):
        far_each(lambda face, other, device: far_copy(round_index, face, other, device).start())

    def far_wait(round_index):
        far_each(
            lambda face, other, device: far_copy(
                round_index, other ^ 1, face ^ 1, device
            ).wait_recv()
        )

    def send_coarse(round_index, sem_row):
        for face in range(4):
            coarse_trace_to(w, owner[face], face, c_send.at[round_index, face])
        start_all(c_send, c_recv, round_index, sem_row)
        far_start(round_index)
        for face in range(4):
            far_recv[round_index, face, pl.ds(HALO * (face ^ 1), HALO), :] = c_send[
                round_index, face
            ]

    def send_ahead(round_index, sem_row):
        for face in range(4):
            coarse_trace_to(pre, owner[face], face, p_send.at[round_index, face])
        start_all(p_send, p_recv, round_index, sem_row)

    for e in range(SLOTS):
        loads["rhs", e].wait()
        live = jnp.where(e < counts[0], 1.0, 0.0)
        rhs[e] = rhs[e] * live
        loads["inv", e].wait()
        if e == 2:
            for name in late:
                loads[name].start()
        left_d[e] = pack_left(0.8 * inv_stage[e])
        v[e] = product(left_d[e], pack_right(rhs[e]))
    pl.semaphore_wait(barrier, peers)
    send_fine(0, 0)

    loads["lifts"].wait()
    loads["coefs"].wait()
    flat = pad_rows(jnp.concatenate([lifts[f] for f in range(6)], axis=0), 512)
    upright = jnp.transpose(pad_lanes(flat, 384))[:NF]
    lift_high, lift_low = halves(upright)
    lift_h[...] = lift_high
    lift_l[...] = lift_low
    coef_sq[...] = jnp.zeros((128, 128), f32)
    for f in range(6):
        coef_sq[pl.ds(8 * f, SLOTS), pl.ds(0, NFACE)] = coefs[f]
    columns = jnp.transpose(coef_sq[...])
    for e in range(SLOTS):
        for f in range(6):
            column = columns[:NFACE, 8 * f + e : 8 * f + e + 1] * local[e, f].astype(f32)
            coef_cols[e, f] = jnp.broadcast_to(column, (NFACE, RHS))
    x_h[pl.ds(480, 32), :] = jnp.zeros((32, SLOTS * RHS), bf16)
    x_l[pl.ds(480, 32), :] = jnp.zeros((32, SLOTS * RHS), bf16)
    for e in range(SLOTS):
        loads["blocks", e].wait()
        left_a[e] = pack_left(stage[e])

    def local_residual():
        for e in range(SLOTS):
            for f in range(6):
                high, low = halves(coef_cols[e, f] * trace(v, slot[e, f], f ^ 1))
                x_h[pl.ds(NFACE * f, NFACE), pl.ds(RHS * e, RHS)] = high
                x_l[pl.ds(NFACE * f, NFACE), pl.ds(RHS * e, RHS)] = low
        for pair in range(2):
            cols = pl.ds(256 * pair, 256)
            coupled = (
                jnp.dot(lift_h[...], x_h[:, cols], preferred_element_type=f32)
                + jnp.dot(lift_h[...], x_l[:, cols], preferred_element_type=f32)
                + jnp.dot(lift_l[...], x_h[:, cols], preferred_element_type=f32)
            )
            for half in range(2):
                e = 2 * pair + half
                block = product(left_a[e], pack_right(v[e]))
                r_loc[e] = rhs[e] - block - coupled[:, 128 * half : 128 * half + 128]

    def presweep():
        for e in range(SLOTS):
            vpre[e] = v[e] + product(left_d[e], pack_right(r_loc[e]))

    def cross_terms(left, recv):
        return [product(left[f], twice(recv[f], 128)) for f in range(4)]

    def combine(terms, src, dst):
        for e in range(SLOTS):
            total = src[e]
            for f in range(4):
                total = total - weight[e, f] * terms[f]
            dst[e] = total

    local_residual()
    presweep()
    scaled = []
    for f in range(4):
        coef_row = sum(weight[e, f] * coefs[f, pl.ds(e, 1), :] for e in range(SLOTS))
        square = jnp.transpose(pad_lanes(pad_rows(lifts[f], 128), 384))[:NF]
        scaled.append(square * pad_lanes(coef_row, 128))
    rights = [pack_right(s) for s in scaled]
    for f in range(4):
        high, low = halves(product(left_d[owner[f]], rights[f]))
        cross_l[f] = jnp.concatenate([high, low], axis=1)

    wait_all(f_send, f_recv, 0, 0)
    combine(cross_terms(cross_l, f_recv.at[0]), vpre, v)
    send_fine(1, 1)

    local_residual()
    for name in ("cblocks", "cinv", "clifts", "ccoefs", "lift", "restrict", "face"):
        loads[name].wait()
    for e in range(SLOTS):
        left_ip[e] = pack_left(
            jnp.dot(0.2 * cinv[e], restrict_tab[...], precision=highest, preferred_element_type=f32)
        )
    for f in range(4):
        high, low = halves(product(left_ip[owner[f]], rights[f]))
        cross_k[f] = jnp.concatenate([high, low], axis=1)
    for e in range(SLOTS):
        w1[e] = product(left_ip[e], pack_right(r_loc[e]))
    clift_sq = [
        jnp.transpose(pad_lanes(pad_rows(clifts[f], 128), 128))[:NC] for f in range(6)
    ]
    t = lax.broadcasted_iota(jnp.int32, (128, 256), 0)
    lane = lax.broadcasted_iota(jnp.int32, (128, 256), 1)
    for e in range(SLOTS):
        def placed(matrix, target):
            high, low = halves(matrix)
            both = jnp.concatenate([high, low], axis=0)
            chosen = jnp.where(lane == target, 1.0, 0.0).astype(bf16)
            out = jnp.dot(both, chosen, preferred_element_type=f32)
            return out[:NC] + out[NC:]

        total = placed(pad_lanes(cblocks[e], 128), jnp.where(t < NC, t + 4 * HALO + NC * e, -1))
        for f in range(6):
            target = local[e, f] * (coarse_rows(f ^ 1, t) + 4 * HALO + NC * slot[e, f] + 1)
            if f < 4:
                target = target + cross[e, f] * (halo_rows(f, t) + HALO * f + 1)
            target = jnp.where(t < NCF, target - 1, -1)
            total = total + placed(clift_sq[f] * pad_lanes(ccoefs[f, pl.ds(e, 1), :], 128), target)
        row = lax.broadcasted_iota(jnp.int32, (NC, 256), 0)
        col = lax.broadcasted_iota(jnp.int32, (NC, 256), 1)
        unit = jnp.where(col == row + 4 * HALO + NC * e, 1.0, 0.0)
        full = unit - jnp.dot(
            0.8 * cinv[e], total, precision=highest, preferred_element_type=f32
        )
        coarse_m[e] = full
        coarse_h[e] = full[:, :128]
    for face in range(4):
        coarse_trace_to(coarse_h, owner[face], face, o_send.at[face])
        @pl.when(sides[face][0])
        def _():
            op_copy(face, face ^ 1).start()

    wait_all(f_send, f_recv, 1, 1)
    combine(cross_terms(cross_k, f_recv.at[1]), w1, w)
    for e in range(SLOTS):
        w1[e] = w[e]
    send_coarse(0, 2)

    left_high, left_low = halves(coarse_m[...].reshape(SLOTS * NC, 256))
    left_m = jnp.concatenate([left_high, left_low], axis=0)

    def quarters(left, right):
        high, low = halves(right)
        moved = jnp.dot(left, jnp.concatenate([high, low], axis=1), preferred_element_type=f32)
        rows = left.shape[0] // 2
        return moved[:rows, :128] + (moved[:rows, 128:] + moved[rows:, :128])

    def local_ahead(sem_row, round_index):
        state = jnp.concatenate(
            [jnp.zeros((4 * HALO, RHS), f32), w[...].reshape(SLOTS * NC, RHS)], axis=0
        )
        pre[...] = w1[...] + quarters(left_m, state).reshape(SLOTS, NC, RHS)
        send_ahead(round_index, sem_row)

    local_ahead(4, 0)
    for f, term in enumerate(cross_terms(cross_l, f_recv.at[1])):
        z_old[f] = term
    for f in range(4):
        high, low = halves(product(cross_l[f], face_tab[f]))
        cross_g[f] = jnp.concatenate([high, low], axis=1)
    for face in range(4):
        @pl.when(sides[face][0])
        def _():
            op_copy(face, face).wait_recv()
    blank = jnp.zeros((HALO, 128), f32)
    keep = lax.broadcasted_iota(jnp.int32, (HALO, 128), 1) < 4 * HALO
    op_rows = []
    for face in range(4):
        block = jnp.where(keep, o_recv[face], 0.0)
        op_rows.append(
            jnp.concatenate([block if k == face else blank for k in range(4)], axis=1)
        )
    op_high, op_low = halves(jnp.concatenate(op_rows, axis=0))
    op_left = jnp.concatenate([op_high, op_low], axis=0)

    def two_steps(round_index, near_row, ahead_row):
        wait_all(c_send, c_recv, round_index, near_row)
        first = quarters(
            left_m[:, :128], pad_rows(c_recv[round_index].reshape(4 * HALO, RHS), 128)
        )
        middle = pre[...].reshape(SLOTS * NC, RHS) + first
        wait_all(p_send, p_recv, round_index, ahead_row)
        far_wait(round_index)
        halo = p_recv[round_index].reshape(4 * HALO, RHS) + quarters(
            op_left, far_recv[round_index].reshape(512, RHS)
        )
        return middle, halo

    middle, halo = two_steps(0, 2, 4)
    ahead = quarters(left_m, jnp.concatenate([halo, middle], axis=0))
    w[...] = w1[...] + ahead.reshape(SLOTS, NC, RHS)
    send_coarse(1, 3)
    local_ahead(5, 1)
    middle, halo = two_steps(1, 3, 5)
    w[...] = middle.reshape(SLOTS, NC, RHS)

    for e in range(SLOTS):
        v[e] = v[e] + product(lift_tab[...], twice(w[e], 64))
    local_residual()
    presweep()
    combine([z_old[f] for f in range(4)], vpre, vpre)
    last = [halo[HALO * f : HALO * f + HALO] for f in range(4)]
    combine(cross_terms(cross_g, last), vpre, v)
    send_fine(2, 6)
    local_residual()
    presweep()
    wait_all(f_send, f_recv, 2, 6)
    combine(cross_terms(cross_l, f_recv.at[2]), vpre, out)

    for face in range(4):
        @pl.when(sides[face][0])
        def _():
            for r, row in ((0, 0), (1, 1), (2, 6)):
                transfer(f_send, f_recv, r, row, face, face ^ 1).wait_send()
            for r in range(2):
                transfer(c_send, c_recv, r, 2 + r, face, face ^ 1).wait_send()
                transfer(p_send, p_recv, r, 4 + r, face, face ^ 1).wait_send()
            op_copy(face, face ^ 1).wait_send()
    for r in range(2):
        far_each(lambda face, other, device: far_copy(r, face, other, device).wait_send())


def body(*args):
    args = list(args)
    for i in (3, 7):
        args[i] = jnp.transpose(args[i], (0, 2, 1))
    for i in (4, 8):
        args[i] = jnp.transpose(args[i], (1, 0, 2))
    any_spec = pl.BlockSpec(memory_space=pltpu.HBM)
    constants = [jnp.asarray(c) for c in tables()]
    pin = lambda x: pltpu.with_memory_space_constraint(x, pltpu.HBM)
    args = [pin(a) for a in args[:10]] + args[10:]
    constants = [pin(c) for c in constants]
    vm = pltpu.VMEM
    scratch = [
        vm((SLOTS, NF, RHS), f32), vm((SLOTS, NF, NF), f32), vm((SLOTS, NF, NF), f32),
        vm((6, NFACE, NF), f32), vm((6, SLOTS, NFACE), f32),
        vm((SLOTS, NC, NC), f32), vm((SLOTS, NC, NC), f32), vm((6, NCF, NC), f32),
        vm((6, SLOTS, NCF), f32),
        vm((NF, 128), bf16), vm((NC, NF), f32), vm((4, 256, 256), bf16),
        vm((SLOTS, NF, 640), bf16), vm((SLOTS, NF, 640), bf16),
        vm((NF, 512), bf16), vm((NF, 512), bf16),
        vm((SLOTS, 6, NFACE, RHS), f32), vm((128, 128), f32),
        vm((SLOTS, NF, RHS), f32), vm((SLOTS, NF, RHS), f32),
        vm((512, 512), bf16), vm((512, 512), bf16), vm((SLOTS, NF, RHS), f32),
        vm((4, NF, 256), bf16), vm((4, NF, 256), bf16), vm((4, NC, 256), bf16),
        vm((SLOTS, NC, 640), bf16), vm((SLOTS, NC, 256), f32),
        vm((SLOTS, NC, RHS), f32), vm((SLOTS, NC, RHS), f32),
        vm((4, NF, RHS), f32),
        vm((3, 4, NFACE, RHS), f32), vm((3, 4, NFACE, RHS), f32),
        vm((2, 4, HALO, RHS), f32), vm((2, 4, HALO, RHS), f32),
        vm((2, 4, 128, RHS), f32),
        vm((2, 4, HALO, RHS), f32), vm((2, 4, HALO, RHS), f32),
        vm((4, HALO, RHS), f32), vm((4, HALO, RHS), f32),
        vm((SLOTS, NC, 128), f32), vm((SLOTS, NC, RHS), f32),
        pltpu.SMEM((SLOTS, 6), jnp.int32),
        pltpu.SemaphoreType.DMA((24,)),
        pltpu.SemaphoreType.DMA((8, 4)), pltpu.SemaphoreType.DMA((8, 4)),
        pltpu.SemaphoreType.DMA((2, 4, 4)), pltpu.SemaphoreType.DMA((2, 4, 4)),
    ]
    return pl.pallas_call(
        kernel,
        out_shape=jax.ShapeDtypeStruct((SLOTS, NF, RHS), f32),
        in_specs=[any_spec] * 10 + [pl.BlockSpec(memory_space=pltpu.SMEM)] + [any_spec] * 3,
        out_specs=pl.BlockSpec(memory_space=pltpu.VMEM),
        scratch_shapes=scratch,
        compiler_params=pltpu.CompilerParams(collective_id=0, has_side_effects=True, vmem_limit_bytes=32 << 20),
        name="cycle",
    )(*args, *constants)


def solution(mesh):
    split = ("wide", "narrow")
    placed = (
        P(split, None, None),
        P(split, None, None),
        P(split, None, None),
        P(),
        P(split, None, None),
        P(split, None, None),
        P(split, None, None),
        P(),
        P(split, None, None),
        P(split, None),
        P(split),
    )
    return jax.shard_map(
        body, mesh=mesh, in_specs=placed, out_specs=P(split, None, None), check_vma=False
    )
```

```python
import jax
import jax.numpy as jnp
import numpy as np
from jax import lax
from jax.experimental import pallas as pl
from jax.experimental.pallas import tpu as pltpu
from jax.sharding import PartitionSpec as P

NVAR = 5
SLOTS = 4
NF = 320
NFACE = 80
NC = 40
NCF = 20
HALO = 24
RHS = 128
WIDE = 8
NARROW = 32
MESH = pl.DeviceIdType.MESH
highest = lax.Precision.HIGHEST
STEPS = [(-1, 0), (1, 0), (0, -1), (0, 1)]
REACH = STEPS + [(-2, 0), (2, 0), (0, -2), (0, 2), (-1, -1), (-1, 1), (1, -1), (1, 1)]
bf16 = jnp.bfloat16
f32 = jnp.float32


def offset(face, other):
    return tuple(a + b for a, b in zip(STEPS[face], STEPS[other]))


def linear_table():
    points = np.array([-1.0, -1.0 / np.sqrt(5.0), 1.0 / np.sqrt(5.0), 1.0])
    return np.stack([(1.0 - points) / 2.0, (1.0 + points) / 2.0], axis=1)


def split_np(values):
    values = values.astype(np.float32)
    high = values.astype(bf16)
    low = (values - high.astype(np.float32)).astype(bf16)
    return high, low


def tables():
    linear = linear_table()
    cube = np.kron(np.kron(linear, linear), linear)
    prolong = np.kron(np.eye(NVAR), cube).astype(np.float32)
    flat = np.kron(np.eye(NVAR), np.kron(linear, linear)).astype(np.float32)
    high, low = split_np(prolong)
    lift = np.zeros((NF, 128), high.dtype)
    lift[:, :NC] = high
    lift[:, 64 : 64 + NC] = low
    high, low = split_np(flat)
    face_tab = np.zeros((2 * NFACE, 128), high.dtype)
    face_tab[:NFACE, :NCF] = high
    face_tab[NFACE:, :NCF] = low
    return lift, np.ascontiguousarray(prolong.T), face_tab


def halves(x):
    high = x.astype(bf16)
    low = (x - high.astype(f32)).astype(bf16)
    return high, low


def pack_left(x):
    high, low = halves(x)
    return jnp.concatenate(
        [high[:, :256], low[:, :256], jnp.concatenate([high[:, 256:], low[:, 256:]], axis=1)],
        axis=1,
    )


def pack_right(x):
    high, low = halves(x)
    both = jnp.concatenate([high, low], axis=1)
    main, rest = both[:256], both[256:]
    return jnp.concatenate([main, main, rest, rest], axis=0)


def product(left, right):
    out = jnp.dot(left, right, preferred_element_type=f32)
    return out[:, :128] + out[:, 128:]


def pad_rows(x, rows):
    return jnp.concatenate([x, jnp.zeros((rows - x.shape[0], x.shape[1]), x.dtype)], axis=0)


def pad_lanes(x, lanes):
    return jnp.concatenate([x, jnp.zeros((x.shape[0], lanes - x.shape[1]), x.dtype)], axis=1)


def twice(x, rows):
    high, low = halves(pad_rows(x, rows))
    both = jnp.concatenate([high, low], axis=1)
    return jnp.concatenate([both, both], axis=0)


def trace(ref, slot, face):
    odd = face & 1
    if face < 2:
        return jnp.concatenate(
            [ref[slot, pl.ds(64 * v + 48 * odd, 16), :] for v in range(NVAR)], axis=0
        )
    if face < 4:
        lanes = ref.shape[-1]
        tiles = ref[slot].reshape(20, 16, lanes)[:, 8 * odd : 8 * odd + 8]
        pairs = tiles.reshape(10, 2, 8, lanes)
        first, second = pairs[:, 0], pairs[:, 1]
        upper = lax.broadcasted_iota(jnp.int32, (10, 8, lanes), 1) < 4
        if odd:
            out = jnp.where(upper, pltpu.roll(first, 4, 1), second)
        else:
            out = jnp.where(upper, first, pltpu.roll(second, 4, 1))
        return out.reshape(NFACE, lanes)
    return ref[slot, pl.ds(3 * odd, NFACE, stride=4), :]


def coarse_trace_to(ref, slot, face, out):
    odd = face & 1
    if face < 2:
        for q in range(4):
            out[pl.ds(5 * q, 5), :] = ref[slot, pl.ds(4 * odd + q, 5, stride=8), :]
    else:
        for q in range(2):
            out[pl.ds(10 * q, 10), :] = ref[slot, pl.ds(2 * odd + q, 10, stride=4), :]


def coarse_rows(face, t):
    odd = face & 1
    var = lax.shift_right_logical(t, 2)
    a = lax.shift_right_logical(t, 1) & 1
    b = t & 1
    if face < 2:
        return var * 8 + 4 * odd + a * 2 + b
    if face < 4:
        return var * 8 + a * 4 + 2 * odd + b
    return var * 8 + a * 4 + b * 2 + odd


def halo_rows(face, t):
    if face < 2:
        return (t & 3) * 5 + lax.shift_right_logical(t, 2)
    return (t & 1) * 10 + lax.shift_right_logical(t, 1)


def kernel(
    rhs_hbm, blocks_hbm, inv_hbm, lifts_hbm, coefs_hbm,
    cblocks_hbm, cinv_hbm, clifts_hbm, ccoefs_hbm, nbr_hbm, counts,
    lift_hbm, restrict_hbm, face_hbm,
    out,
    rhs, stage, inv_stage, lifts, coefs, cblocks, cinv, clifts, ccoefs, lift_tab, restrict_tab, face_tab,
    left_a, left_d, lift_h, lift_l, coef_cols, coef_sq,
    v, vpre, x_h, x_l, r_loc, cross_l, left_r, full_r, coef_raw, cross_k, left_ip, coarse_m, w1, w,
    f_send, f_recv, c_send, c_recv, far_recv, p_send, p_recv, o_send, o_recv, coarse_h, pre,
    nbr, load_sem, send_sem, recv_sem, far_send_sem, far_recv_sem,
):
    wide = lax.axis_index("wide")
    narrow = lax.axis_index("narrow")
    base = (wide * NARROW + narrow) * SLOTS

    def inside(dw, dn):
        conditions = []
        if dw < 0:
            conditions.append(wide >= -dw)
        if dw > 0:
            conditions.append(wide < WIDE - dw)
        if dn < 0:
            conditions.append(narrow >= -dn)
        if dn > 0:
            conditions.append(narrow < NARROW - dn)
        result = conditions[0]
        for condition in conditions[1:]:
            result = jnp.logical_and(result, condition)
        return result

    def place(dw, dn):
        return (wide + dw, narrow + dn)

    sides = [(inside(*STEPS[face]), place(*STEPS[face])) for face in range(4)]

    barrier = pltpu.get_barrier_semaphore()
    peers = 0
    for dw, dn in REACH:
        has = inside(dw, dn)
        peers = peers + jnp.where(has, 1, 0)

        @pl.when(has)
        def _():
            pl.semaphore_signal(barrier, 1, device_id=place(dw, dn), device_id_type=MESH)

    loads = {}
    count = 0
    pairs = [("nbr", nbr_hbm, nbr)]
    pairs += [(("rhs", e), rhs_hbm.at[e], rhs.at[e]) for e in range(SLOTS)]
    pairs += [(("inv", e), inv_hbm.at[e], inv_stage.at[e]) for e in range(SLOTS)]
    pairs += [("lifts", lifts_hbm, lifts), ("coefs", coefs_hbm, coefs)]
    pairs += [(("blocks", e), blocks_hbm.at[e], stage.at[e]) for e in range(SLOTS)]
    pairs += [
        ("cblocks", cblocks_hbm, cblocks), ("cinv", cinv_hbm, cinv),
        ("clifts", clifts_hbm, clifts), ("ccoefs", ccoefs_hbm, ccoefs),
        ("lift", lift_hbm, lift_tab), ("restrict", restrict_hbm, restrict_tab),
        ("face", face_hbm, face_tab),
    ]
    for name, src, dst in pairs:
        loads[name] = pltpu.make_async_copy(src, dst, load_sem.at[count])
        count += 1
    early = ["nbr"]
    for e in range(SLOTS):
        early += [("rhs", e), ("inv", e)]
    late = [name for name in loads if name not in early]
    first = early
    for name in first:
        loads[name].start()

    for face in range(4):
        @pl.when(jnp.logical_not(sides[face][0]))
        def _():
            for r in range(3):
                f_recv[r, face] = jnp.zeros((NFACE, RHS), f32)
            for r in range(2):
                c_recv[r, face] = jnp.zeros((HALO, RHS), f32)
                p_recv[r, face] = jnp.zeros((HALO, RHS), f32)
            o_recv[face] = jnp.zeros((HALO, RHS), f32)
    tail = jnp.zeros((8, RHS), f32)
    for face in range(4):
        for r in range(2):
            c_send[r, face, pl.ds(16, 8), :] = tail
            p_send[r, face, pl.ds(16, 8), :] = tail
            far_recv[r, face, pl.ds(4 * HALO, 32), :] = jnp.zeros((32, RHS), f32)
        o_send[face, pl.ds(16, 8), :] = tail
        for other in range(4):
            if other != face ^ 1:
                @pl.when(jnp.logical_not(inside(*offset(face, other))))
                def _():
                    for r in range(2):
                        far_recv[r, face, pl.ds(HALO * other, HALO), :] = jnp.zeros((HALO, RHS), f32)

    for name in early:
        if name not in first:
            loads[name].start()
    loads["nbr"].wait()
    local, slot, cross = {}, {}, {}
    for e in range(SLOTS):
        for f in range(6):
            g = nbr[e, f]
            here = jnp.logical_and(g >= base, g < base + SLOTS)
            local[e, f] = jnp.where(here, 1, 0)
            slot[e, f] = jnp.clip(g - base, 0, SLOTS - 1)
            if f < 4:
                cross[e, f] = jnp.where(jnp.logical_and(g >= 0, jnp.logical_not(here)), 1, 0)
    owner = [
        jnp.clip(sum(e * cross[e, f] for e in range(1, SLOTS)), 0, SLOTS - 1) for f in range(4)
    ]
    weight = {key: value.astype(f32) for key, value in cross.items()}

    def transfer(send, recv, round_index, sem_row, face, target):
        return pltpu.make_async_remote_copy(
            src_ref=send.at[round_index, face],
            dst_ref=recv.at[round_index, target],
            send_sem=send_sem.at[sem_row, face],
            recv_sem=recv_sem.at[sem_row, target],
            device_id=sides[face][1],
            device_id_type=MESH,
        )

    def start_all(send, recv, round_index, sem_row):
        for face in range(4):
            @pl.when(sides[face][0])
            def _():
                transfer(send, recv, round_index, sem_row, face, face ^ 1).start()

    def wait_all(send, recv, round_index, sem_row):
        for face in range(4):
            @pl.when(sides[face][0])
            def _():
                transfer(send, recv, round_index, sem_row, face, face).wait_recv()

    def op_copy(face, target):
        return pltpu.make_async_remote_copy(
            src_ref=o_send.at[face],
            dst_ref=o_recv.at[target],
            send_sem=send_sem.at[7, face],
            recv_sem=recv_sem.at[7, target],
            device_id=sides[face][1],
            device_id_type=MESH,
        )

    def send_fine(round_index, sem_row):
        for face in range(4):
            f_send[round_index, face] = trace(v, owner[face], face)
        start_all(f_send, f_recv, round_index, sem_row)

    def far_copy(round_index, face, other, device):
        return pltpu.make_async_remote_copy(
            src_ref=c_send.at[round_index, face],
            dst_ref=far_recv.at[round_index, other ^ 1, pl.ds(HALO * (face ^ 1), HALO)],
            send_sem=far_send_sem.at[round_index, face, other],
            recv_sem=far_recv_sem.at[round_index, other ^ 1, face ^ 1],
            device_id=device,
            device_id_type=MESH,
        )

    def far_each(act):
        turns = [(a, b) for a in range(4) for b in range(4) if a // 2 != b // 2]
        for face, other in turns + [(a, a) for a in range(4)]:
            @pl.when(inside(*offset(face, other)))
            def _():
                act(face, other, place(*offset(face, other)))

    def far_start(round_index):
        far_each(lambda face, other, device: far_copy(round_index, face, other, device).start())

    def far_wait(round_index):
        far_each(
            lambda face, other, device: far_copy(
                round_index, other ^ 1, face ^ 1, device
            ).wait_recv()
        )

    def send_coarse(round_index, sem_row):
        for face in range(4):
            coarse_trace_to(w, owner[face], face, c_send.at[round_index, face])
        far_start(round_index)
        start_all(c_send, c_recv, round_index, sem_row)
        for face in range(4):
            far_recv[round_index, face, pl.ds(HALO * (face ^ 1), HALO), :] = c_send[
                round_index, face
            ]

    def send_ahead(round_index, sem_row):
        for face in range(4):
            coarse_trace_to(pre, owner[face], face, p_send.at[round_index, face])
        start_all(p_send, p_recv, round_index, sem_row)

    for e in range(SLOTS):
        loads["rhs", e].wait()
        live = jnp.where(e < counts[0], 1.0, 0.0)
        rhs[e] = rhs[e] * live
        loads["inv", e].wait()
        if e == 2:
            for name in late:
                loads[name].start()
        left_d[e] = pack_left(0.8 * inv_stage[e])
        v[e] = product(left_d[e], pack_right(rhs[e]))
    pl.semaphore_wait(barrier, peers)
    send_fine(0, 0)

    loads["lifts"].wait()
    loads["coefs"].wait()
    flat = pad_rows(jnp.concatenate([lifts[f] for f in range(6)], axis=0), 512)
    upright = jnp.transpose(pad_lanes(flat, 384))[:NF]
    lift_high, lift_low = halves(upright)
    lift_h[...] = lift_high
    lift_l[...] = lift_low
    coef_sq[...] = jnp.zeros((128, 128), f32)
    for f in range(6):
        coef_sq[pl.ds(8 * f, SLOTS), pl.ds(0, NFACE)] = coefs[f]
    columns = jnp.transpose(coef_sq[...])
    for e in range(SLOTS):
        for f in range(6):
            column = columns[:NFACE, 8 * f + e : 8 * f + e + 1]
            column = jnp.broadcast_to(column, (NFACE, RHS))
            coef_raw[e, f] = column
            coef_cols[e, f] = column * local[e, f].astype(f32)
    x_h[pl.ds(480, 32), :] = jnp.zeros((32, SLOTS * RHS), bf16)
    x_l[pl.ds(480, 32), :] = jnp.zeros((32, SLOTS * RHS), bf16)
    for e in range(SLOTS):
        loads["blocks", e].wait()
        left_a[e] = pack_left(stage[e])

    def local_residual():
        for e in range(SLOTS):
            for f in range(6):
                high, low = halves(coef_cols[e, f] * trace(v, slot[e, f], f ^ 1))
                x_h[pl.ds(NFACE * f, NFACE), pl.ds(RHS * e, RHS)] = high
                x_l[pl.ds(NFACE * f, NFACE), pl.ds(RHS * e, RHS)] = low
        for pair in range(2):
            cols = pl.ds(256 * pair, 256)
            coupled = (
                jnp.dot(lift_h[...], x_h[:, cols], preferred_element_type=f32)
                + jnp.dot(lift_h[...], x_l[:, cols], preferred_element_type=f32)
                + jnp.dot(lift_l[...], x_h[:, cols], preferred_element_type=f32)
            )
            for half in range(2):
                e = 2 * pair + half
                block = product(left_a[e], pack_right(v[e]))
                r_loc[e] = rhs[e] - block - coupled[:, 128 * half : 128 * half + 128]

    def presweep(which=range(SLOTS)):
        for e in which:
            vpre[e] = v[e] + product(left_d[e], pack_right(r_loc[e]))

    def cross_terms(left, recv):
        return [product(left[f], twice(recv[f], 128)) for f in range(4)]

    def combine(terms, src, dst):
        for e in range(SLOTS):
            total = src[e]
            for f in range(4):
                total = total - weight[e, f] * terms[f]
            dst[e] = total

    local_residual()
    presweep()
    scaled = []
    for f in range(4):
        coef_row = sum(weight[e, f] * coefs[f, pl.ds(e, 1), :] for e in range(SLOTS))
        square = jnp.transpose(pad_lanes(pad_rows(lifts[f], 128), 384))[:NF]
        scaled.append(square * pad_lanes(coef_row, 128))
    rights = [pack_right(s) for s in scaled]
    for f in range(4):
        high, low = halves(product(left_d[owner[f]], rights[f]))
        cross_l[f] = jnp.concatenate([high, low], axis=1)

    wait_all(f_send, f_recv, 0, 0)
    combine(cross_terms(cross_l, f_recv.at[0]), vpre, v)
    send_fine(1, 1)

    local_residual()
    for name in ("cblocks", "cinv", "clifts", "ccoefs", "lift", "restrict", "face"):
        loads[name].wait()
    for e in range(SLOTS):
        left_ip[e] = pack_left(
            jnp.dot(0.2 * cinv[e], restrict_tab[...], precision=highest, preferred_element_type=f32)
        )
    for f in range(4):
        high, low = halves(product(left_ip[owner[f]], rights[f]))
        cross_k[f] = jnp.concatenate([high, low], axis=1)
    for e in range(SLOTS):
        w1[e] = product(left_ip[e], pack_right(r_loc[e]))
    clift_sq = [
        jnp.transpose(pad_lanes(pad_rows(clifts[f], 128), 128))[:NC] for f in range(6)
    ]

    def one_hot(rows, make):
        t = lax.broadcasted_iota(jnp.int32, (rows, 256), 0)
        lane = lax.broadcasted_iota(jnp.int32, (rows, 256), 1)
        return jnp.where(lane == make(t), 1.0, 0.0).astype(bf16)

    def face_target(e, f):
        def make(t):
            target = local[e, f] * (coarse_rows(f ^ 1, t) + 4 * HALO + NC * slot[e, f] + 1)
            if f < 4:
                target = target + cross[e, f] * (halo_rows(f, t) + HALO * f + 1)
            return jnp.where(t < NCF, target - 1, -1)

        return one_hot(32, make)

    def placed(matrix, chosen):
        high, low = halves(matrix)
        out = jnp.dot(
            jnp.concatenate([high, low], axis=0), chosen, preferred_element_type=f32
        )
        return out[:NC] + out[NC:]

    for e in range(SLOTS):
        start = 4 * HALO + NC * e
        total = placed(
            pad_lanes(cblocks[e], 128), one_hot(128, lambda t: jnp.where(t < NC, t + start, -1))
        )
        for f in range(6):
            scaled_lift = clift_sq[f] * pad_lanes(ccoefs[f, pl.ds(e, 1), :], 128)
            total = total + placed(scaled_lift[:, :32], face_target(e, f))
        row = lax.broadcasted_iota(jnp.int32, (NC, 256), 0)
        col = lax.broadcasted_iota(jnp.int32, (NC, 256), 1)
        unit = jnp.where(col == row + 4 * HALO + NC * e, 1.0, 0.0)
        full = unit - jnp.dot(
            0.8 * cinv[e], total, precision=highest, preferred_element_type=f32
        )
        coarse_m[e] = full
        coarse_h[e] = full[:, :128]
    for face in range(4):
        coarse_trace_to(coarse_h, owner[face], face, o_send.at[face])
        @pl.when(sides[face][0])
        def _():
            op_copy(face, face ^ 1).start()

    wait_all(f_send, f_recv, 1, 1)
    combine(cross_terms(cross_k, f_recv.at[1]), w1, w)
    for e in range(SLOTS):
        w1[e] = w[e]
    send_coarse(0, 2)

    left_high, left_low = halves(coarse_m[...].reshape(SLOTS * NC, 256))
    left_m = jnp.concatenate([left_high, left_low], axis=0)

    def quarters(left, right):
        high, low = halves(right)
        moved = jnp.dot(left, jnp.concatenate([high, low], axis=1), preferred_element_type=f32)
        rows = left.shape[0] // 2
        return moved[:rows, :128] + (moved[:rows, 128:] + moved[rows:, :128])

    def local_ahead(sem_row, round_index):
        state = jnp.concatenate(
            [jnp.zeros((4 * HALO, RHS), f32), w[...].reshape(SLOTS * NC, RHS)], axis=0
        )
        pre[...] = w1[...] + quarters(left_m, state).reshape(SLOTS, NC, RHS)
        send_ahead(round_index, sem_row)

    local_ahead(4, 0)
    for face in range(4):
        @pl.when(sides[face][0])
        def _():
            op_copy(face, face).wait_recv()
    blank = jnp.zeros((HALO, 128), f32)
    keep = lax.broadcasted_iota(jnp.int32, (HALO, 128), 1) < 4 * HALO
    op_rows = []
    for face in range(4):
        block = jnp.where(keep, o_recv[face], 0.0)
        op_rows.append(
            jnp.concatenate([block if k == face else blank for k in range(4)], axis=1)
        )
    op_full = jnp.concatenate(op_rows, axis=0)
    op_high, op_low = halves(op_full)
    op_left = jnp.concatenate([op_high, op_low], axis=0)

    def wide_product(left, right):
        high, low = halves(right)
        both = jnp.concatenate([high, low], axis=1)
        main, rest = both[:256], both[256:]
        out = jnp.dot(
            left,
            jnp.concatenate([main, main, rest, rest], axis=0),
            preferred_element_type=f32,
        )
        return out[:, :256] + out[:, 256:]

    def correction(pair):
        for half in range(2):
            e = 2 * pair + half
            for f in range(6):
                out = jnp.dot(
                    face_tab[:, :32], face_target(e, f), preferred_element_type=f32
                )
                coef = coef_raw[e, f]
                high, low = halves(
                    (out[:NFACE] + out[NFACE:]) * jnp.concatenate([coef, coef], axis=1)
                )
                x_h[pl.ds(NFACE * f, NFACE), pl.ds(256 * half, 256)] = high
                x_l[pl.ds(NFACE * f, NFACE), pl.ds(256 * half, 256)] = low
        for half in range(2):
            e = 2 * pair + half
            cols = pl.ds(256 * half, 256)
            start = 4 * HALO + NC * e
            coupled = (
                jnp.dot(lift_h[...], x_h[:, cols], preferred_element_type=f32)
                + jnp.dot(lift_h[...], x_l[:, cols], preferred_element_type=f32)
                + jnp.dot(lift_l[...], x_h[:, cols], preferred_element_type=f32)
            )
            chosen = one_hot(
                128, lambda t: jnp.where((t & 63) < NC, (t & 63) + start, -1)
            )
            prolonged = jnp.dot(lift_tab[...], chosen, preferred_element_type=f32)
            coupled = coupled + wide_product(left_a[e], prolonged)
            full = prolonged - wide_product(left_d[e], coupled)
            full_r[e] = full
            high, low = halves(full)
            left_r[e] = jnp.concatenate([high, low], axis=0)

    correction(0)
    presweep(range(2))

    def one_step(round_index, near_row, ahead_row):
        wait_all(c_send, c_recv, round_index, near_row)
        first = quarters(
            left_m[:, :128], pad_rows(c_recv[round_index].reshape(4 * HALO, RHS), 128)
        )
        middle = pre[...].reshape(SLOTS * NC, RHS) + first
        wait_all(p_send, p_recv, round_index, ahead_row)
        return jnp.concatenate([p_recv[round_index].reshape(4 * HALO, RHS), middle], axis=0)

    state = one_step(0, 2, 4)
    far_wait(0)
    halo = state[: 4 * HALO] + quarters(op_left, far_recv[0].reshape(512, RHS))
    ahead = quarters(left_m, jnp.concatenate([halo, state[4 * HALO :]], axis=0))
    w[...] = w1[...] + ahead.reshape(SLOTS, NC, RHS)
    send_coarse(1, 3)
    local_ahead(5, 1)
    correction(1)
    presweep(range(2, SLOTS))
    combine(cross_terms(cross_l, f_recv.at[1]), vpre, vpre)
    lines = [trace(full_r, owner[face], face) for face in range(4)]
    high, low = halves(jnp.concatenate(lines, axis=0))
    left_t = jnp.concatenate([high, low], axis=0)
    for face in range(4):
        f_send[2, face] = trace(vpre, owner[face], face)

    state = one_step(1, 3, 5)
    far_wait(1)
    halo = state[: 4 * HALO] + quarters(op_left, far_recv[1].reshape(512, RHS))
    high, low = halves(jnp.concatenate([halo, state[4 * HALO :]], axis=0))
    state = jnp.concatenate([high, low], axis=1)

    def moved_by(left):
        rows = left.shape[0] // 2
        moved = jnp.dot(left, state, preferred_element_type=f32)
        return moved[:rows, :128] + (moved[:rows, 128:] + moved[rows:, :128])

    moved = moved_by(left_t)
    for face in range(4):
        f_send[2, face] = f_send[2, face] + moved[NFACE * face : NFACE * face + NFACE]
    start_all(f_send, f_recv, 2, 6)
    for e in range(SLOTS):
        v[e] = vpre[e] + moved_by(left_r[e])
    local_residual()
    presweep()
    wait_all(f_send, f_recv, 2, 6)
    combine(cross_terms(cross_l, f_recv.at[2]), vpre, out)

    for face in range(4):
        @pl.when(sides[face][0])
        def _():
            for r, row in ((0, 0), (1, 1), (2, 6)):
                transfer(f_send, f_recv, r, row, face, face ^ 1).wait_send()
            for r in range(2):
                transfer(c_send, c_recv, r, 2 + r, face, face ^ 1).wait_send()
                transfer(p_send, p_recv, r, 4 + r, face, face ^ 1).wait_send()
            op_copy(face, face ^ 1).wait_send()
    for r in range(2):
        far_each(lambda face, other, device: far_copy(r, face, other, device).wait_send())


def body(*args):
    args = list(args)
    for i in (3, 7):
        args[i] = jnp.transpose(args[i], (0, 2, 1))
    for i in (4, 8):
        args[i] = jnp.transpose(args[i], (1, 0, 2))
    any_spec = pl.BlockSpec(memory_space=pltpu.HBM)
    constants = [jnp.asarray(c) for c in tables()]
    pin = lambda x: pltpu.with_memory_space_constraint(x, pltpu.HBM)
    args = [pin(a) for a in args[:10]] + args[10:]
    constants = [pin(c) for c in constants]
    vm = pltpu.VMEM
    scratch = [
        vm((SLOTS, NF, RHS), f32), vm((SLOTS, NF, NF), f32), vm((SLOTS, NF, NF), f32),
        vm((6, NFACE, NF), f32), vm((6, SLOTS, NFACE), f32),
        vm((SLOTS, NC, NC), f32), vm((SLOTS, NC, NC), f32), vm((6, NCF, NC), f32),
        vm((6, SLOTS, NCF), f32),
        vm((NF, 128), bf16), vm((NC, NF), f32), vm((2 * NFACE, 128), bf16),
        vm((SLOTS, NF, 640), bf16), vm((SLOTS, NF, 640), bf16),
        vm((NF, 512), bf16), vm((NF, 512), bf16),
        vm((SLOTS, 6, NFACE, RHS), f32), vm((128, 128), f32),
        vm((SLOTS, NF, RHS), f32), vm((SLOTS, NF, RHS), f32),
        vm((512, 512), bf16), vm((512, 512), bf16), vm((SLOTS, NF, RHS), f32),
        vm((4, NF, 256), bf16), vm((SLOTS, 2 * NF, 256), bf16), vm((SLOTS, NF, 256), f32), vm((SLOTS, 6, NFACE, RHS), f32), vm((4, NC, 256), bf16),
        vm((SLOTS, NC, 640), bf16), vm((SLOTS, NC, 256), f32),
        vm((SLOTS, NC, RHS), f32), vm((SLOTS, NC, RHS), f32),
        vm((3, 4, NFACE, RHS), f32), vm((3, 4, NFACE, RHS), f32),
        vm((2, 4, HALO, RHS), f32), vm((2, 4, HALO, RHS), f32),
        vm((2, 4, 128, RHS), f32),
        vm((2, 4, HALO, RHS), f32), vm((2, 4, HALO, RHS), f32),
        vm((4, HALO, RHS), f32), vm((4, HALO, RHS), f32),
        vm((SLOTS, NC, 128), f32), vm((SLOTS, NC, RHS), f32),
        pltpu.SMEM((SLOTS, 6), jnp.int32),
        pltpu.SemaphoreType.DMA((24,)),
        pltpu.SemaphoreType.DMA((8, 4)), pltpu.SemaphoreType.DMA((8, 4)),
        pltpu.SemaphoreType.DMA((2, 4, 4)), pltpu.SemaphoreType.DMA((2, 4, 4)),
    ]
    return pl.pallas_call(
        kernel,
        out_shape=jax.ShapeDtypeStruct((SLOTS, NF, RHS), f32),
        in_specs=[any_spec] * 10 + [pl.BlockSpec(memory_space=pltpu.SMEM)] + [any_spec] * 3,
        out_specs=pl.BlockSpec(memory_space=pltpu.VMEM),
        scratch_shapes=scratch,
        compiler_params=pltpu.CompilerParams(collective_id=0, has_side_effects=True, vmem_limit_bytes=32 << 20),
        name="cycle",
    )(*args, *constants)


def solution(mesh):
    split = ("wide", "narrow")
    placed = (
        P(split, None, None),
        P(split, None, None),
        P(split, None, None),
        P(),
        P(split, None, None),
        P(split, None, None),
        P(split, None, None),
        P(),
        P(split, None, None),
        P(split, None),
        P(split),
    )
    return jax.shard_map(
        body, mesh=mesh, in_specs=placed, out_specs=P(split, None, None), check_vma=False
    )
```

```python
import jax
import jax.numpy as jnp
import numpy as np
from jax import lax
from jax.experimental import pallas as pl
from jax.experimental.pallas import tpu as pltpu
from jax.sharding import PartitionSpec as P

NVAR = 5
SLOTS = 4
NF = 320
NFACE = 80
NC = 40
NCF = 20
HALO = 24
RHS = 128
WIDE = 8
NARROW = 32
MESH = pl.DeviceIdType.MESH
highest = lax.Precision.HIGHEST
STEPS = [(-1, 0), (1, 0), (0, -1), (0, 1)]
REACH = STEPS + [(-2, 0), (2, 0), (0, -2), (0, 2), (-1, -1), (-1, 1), (1, -1), (1, 1)]
bf16 = jnp.bfloat16
f32 = jnp.float32


def offset(face, other):
    return tuple(a + b for a, b in zip(STEPS[face], STEPS[other]))


def linear_table():
    points = np.array([-1.0, -1.0 / np.sqrt(5.0), 1.0 / np.sqrt(5.0), 1.0])
    return np.stack([(1.0 - points) / 2.0, (1.0 + points) / 2.0], axis=1)


def split_np(values):
    values = values.astype(np.float32)
    high = values.astype(bf16)
    low = (values - high.astype(np.float32)).astype(bf16)
    return high, low


def tables():
    linear = linear_table()
    cube = np.kron(np.kron(linear, linear), linear)
    prolong = np.kron(np.eye(NVAR), cube).astype(np.float32)
    flat = np.kron(np.eye(NVAR), np.kron(linear, linear)).astype(np.float32)
    high, low = split_np(prolong)
    lift = np.zeros((NF, 128), high.dtype)
    lift[:, :NC] = high
    lift[:, 64 : 64 + NC] = low
    high, low = split_np(flat)
    face_tab = np.zeros((2 * NFACE, 128), high.dtype)
    face_tab[:NFACE, :NCF] = high
    face_tab[NFACE:, :NCF] = low
    return lift, np.ascontiguousarray(prolong.T), face_tab


def halves(x):
    high = x.astype(bf16)
    low = (x - high.astype(f32)).astype(bf16)
    return high, low


def pack_left(x):
    high, low = halves(x)
    return jnp.concatenate(
        [high[:, :256], low[:, :256], jnp.concatenate([high[:, 256:], low[:, 256:]], axis=1)],
        axis=1,
    )


def pack_right(x):
    high, low = halves(x)
    both = jnp.concatenate([high, low], axis=1)
    main, rest = both[:256], both[256:]
    return jnp.concatenate([main, main, rest, rest], axis=0)


def product(left, right):
    out = jnp.dot(left, right, preferred_element_type=f32)
    return out[:, :128] + out[:, 128:]


def pad_rows(x, rows):
    return jnp.concatenate([x, jnp.zeros((rows - x.shape[0], x.shape[1]), x.dtype)], axis=0)


def pad_lanes(x, lanes):
    return jnp.concatenate([x, jnp.zeros((x.shape[0], lanes - x.shape[1]), x.dtype)], axis=1)


def twice(x, rows):
    high, low = halves(pad_rows(x, rows))
    both = jnp.concatenate([high, low], axis=1)
    return jnp.concatenate([both, both], axis=0)


def trace(ref, slot, face):
    odd = face & 1
    if face < 2:
        return jnp.concatenate(
            [ref[slot, pl.ds(64 * v + 48 * odd, 16), :] for v in range(NVAR)], axis=0
        )
    if face < 4:
        lanes = ref.shape[-1]
        tiles = ref[slot].reshape(20, 16, lanes)[:, 8 * odd : 8 * odd + 8]
        pairs = tiles.reshape(10, 2, 8, lanes)
        first, second = pairs[:, 0], pairs[:, 1]
        upper = lax.broadcasted_iota(jnp.int32, (10, 8, lanes), 1) < 4
        if odd:
            out = jnp.where(upper, pltpu.roll(first, 4, 1), second)
        else:
            out = jnp.where(upper, first, pltpu.roll(second, 4, 1))
        return out.reshape(NFACE, lanes)
    return ref[slot, pl.ds(3 * odd, NFACE, stride=4), :]


def coarse_trace_to(ref, slot, face, out):
    odd = face & 1
    if face < 2:
        for q in range(4):
            out[pl.ds(5 * q, 5), :] = ref[slot, pl.ds(4 * odd + q, 5, stride=8), :]
    else:
        for q in range(2):
            out[pl.ds(10 * q, 10), :] = ref[slot, pl.ds(2 * odd + q, 10, stride=4), :]


def coarse_rows(face, t):
    odd = face & 1
    var = lax.shift_right_logical(t, 2)
    a = lax.shift_right_logical(t, 1) & 1
    b = t & 1
    if face < 2:
        return var * 8 + 4 * odd + a * 2 + b
    if face < 4:
        return var * 8 + a * 4 + 2 * odd + b
    return var * 8 + a * 4 + b * 2 + odd


def halo_rows(face, t):
    if face < 2:
        return (t & 3) * 5 + lax.shift_right_logical(t, 2)
    return (t & 1) * 10 + lax.shift_right_logical(t, 1)


def kernel(
    rhs_hbm, blocks_hbm, inv_hbm, lifts_hbm, coefs_hbm,
    cblocks_hbm, cinv_hbm, clifts_hbm, ccoefs_hbm, nbr_hbm, counts,
    lift_hbm, restrict_hbm, face_hbm,
    out,
    rhs, stage, inv_stage, lifts, coefs, cblocks, cinv, clifts, ccoefs, lift_tab, restrict_tab, face_tab,
    left_a, left_d, lift_h, lift_l, coef_cols, coef_sq,
    v, vpre, x_h, x_l, r_loc, cross_l, left_r, full_r, coef_raw, cross_k, left_ip, coarse_m, w1, w,
    z, f_send, f_recv, c_send, c_recv, far_recv, p_send, p_recv, o_send, o_recv, coarse_h, pre,
    nbr, load_sem, send_sem, recv_sem, far_send_sem, far_recv_sem,
):
    wide = lax.axis_index("wide")
    narrow = lax.axis_index("narrow")
    base = (wide * NARROW + narrow) * SLOTS

    def inside(dw, dn):
        conditions = []
        if dw < 0:
            conditions.append(wide >= -dw)
        if dw > 0:
            conditions.append(wide < WIDE - dw)
        if dn < 0:
            conditions.append(narrow >= -dn)
        if dn > 0:
            conditions.append(narrow < NARROW - dn)
        result = conditions[0]
        for condition in conditions[1:]:
            result = jnp.logical_and(result, condition)
        return result

    def place(dw, dn):
        return (wide + dw, narrow + dn)

    sides = [(inside(*STEPS[face]), place(*STEPS[face])) for face in range(4)]

    barrier = pltpu.get_barrier_semaphore()
    peers = 0
    for dw, dn in REACH:
        has = inside(dw, dn)
        peers = peers + jnp.where(has, 1, 0)

        @pl.when(has)
        def _():
            pl.semaphore_signal(barrier, 1, device_id=place(dw, dn), device_id_type=MESH)

    loads = {}
    count = 0
    pairs = [("nbr", nbr_hbm, nbr)]
    pairs += [(("rhs", e), rhs_hbm.at[e], rhs.at[e]) for e in range(SLOTS)]
    pairs += [(("inv", e), inv_hbm.at[e], inv_stage.at[e]) for e in range(SLOTS)]
    pairs += [("lifts", lifts_hbm, lifts), ("coefs", coefs_hbm, coefs)]
    pairs += [(("blocks", e), blocks_hbm.at[e], stage.at[e]) for e in range(SLOTS)]
    pairs += [
        ("cblocks", cblocks_hbm, cblocks), ("cinv", cinv_hbm, cinv),
        ("clifts", clifts_hbm, clifts), ("ccoefs", ccoefs_hbm, ccoefs),
        ("lift", lift_hbm, lift_tab), ("restrict", restrict_hbm, restrict_tab),
        ("face", face_hbm, face_tab),
    ]
    for name, src, dst in pairs:
        loads[name] = pltpu.make_async_copy(src, dst, load_sem.at[count])
        count += 1
    early = ["nbr"]
    for e in range(SLOTS):
        early += [("rhs", e), ("inv", e)]
    late = [name for name in loads if name not in early]
    first = early
    for name in first:
        loads[name].start()

    for face in range(4):
        @pl.when(jnp.logical_not(sides[face][0]))
        def _():
            for r in range(3):
                f_recv[r, face] = jnp.zeros((NFACE, RHS), f32)
            for r in range(2):
                c_recv[r, face] = jnp.zeros((HALO, RHS), f32)
                p_recv[r, face] = jnp.zeros((HALO, RHS), f32)
            o_recv[face] = jnp.zeros((HALO, RHS), f32)
    tail = jnp.zeros((8, RHS), f32)
    for face in range(4):
        for r in range(2):
            for other in range(4):
                if other != face ^ 1:
                    far_recv[r, face, pl.ds(HALO * other + NCF, 4), :] = jnp.zeros((4, RHS), f32)
            c_send[r, face, pl.ds(16, 8), :] = tail
            p_send[r, face, pl.ds(16, 8), :] = tail
            far_recv[r, face, pl.ds(4 * HALO, 32), :] = jnp.zeros((32, RHS), f32)
        o_send[face, pl.ds(16, 8), :] = tail
        for other in range(4):
            if other != face ^ 1:
                @pl.when(jnp.logical_not(inside(*offset(face, other))))
                def _():
                    for r in range(2):
                        far_recv[r, face, pl.ds(HALO * other, HALO), :] = jnp.zeros((HALO, RHS), f32)

    for name in early:
        if name not in first:
            loads[name].start()
    loads["nbr"].wait()
    local, slot, cross = {}, {}, {}
    for e in range(SLOTS):
        for f in range(6):
            g = nbr[e, f]
            here = jnp.logical_and(g >= base, g < base + SLOTS)
            local[e, f] = jnp.where(here, 1, 0)
            slot[e, f] = jnp.clip(g - base, 0, SLOTS - 1)
            if f < 4:
                cross[e, f] = jnp.where(jnp.logical_and(g >= 0, jnp.logical_not(here)), 1, 0)
    owner = [
        jnp.clip(sum(e * cross[e, f] for e in range(1, SLOTS)), 0, SLOTS - 1) for f in range(4)
    ]
    weight = {key: value.astype(f32) for key, value in cross.items()}
    shared = {
        (d, f): sum(
            jnp.where(owner[d] == e, 1, 0) * cross[e, f] for e in range(SLOTS)
        ).astype(f32)
        for d in range(4)
        for f in range(4)
    }

    def transfer(send, recv, round_index, sem_row, face, target):
        return pltpu.make_async_remote_copy(
            src_ref=send.at[round_index, face],
            dst_ref=recv.at[round_index, target],
            send_sem=send_sem.at[sem_row, face],
            recv_sem=recv_sem.at[sem_row, target],
            device_id=sides[face][1],
            device_id_type=MESH,
        )

    def start_all(send, recv, round_index, sem_row):
        for face in range(4):
            @pl.when(sides[face][0])
            def _():
                transfer(send, recv, round_index, sem_row, face, face ^ 1).start()

    def wait_all(send, recv, round_index, sem_row):
        for face in range(4):
            @pl.when(sides[face][0])
            def _():
                transfer(send, recv, round_index, sem_row, face, face).wait_recv()

    def op_copy(face, target):
        return pltpu.make_async_remote_copy(
            src_ref=o_send.at[face],
            dst_ref=o_recv.at[target],
            send_sem=send_sem.at[7, face],
            recv_sem=recv_sem.at[7, target],
            device_id=sides[face][1],
            device_id_type=MESH,
        )

    def send_fine(round_index, sem_row):
        for face in range(4):
            f_send[round_index, face] = trace(v, owner[face], face)
        start_all(f_send, f_recv, round_index, sem_row)

    def far_copy(round_index, face, other, device):
        return pltpu.make_async_remote_copy(
            src_ref=c_send.at[round_index, face, pl.ds(0, NCF)],
            dst_ref=far_recv.at[round_index, other ^ 1, pl.ds(HALO * (face ^ 1), NCF)],
            send_sem=far_send_sem.at[round_index, face, other],
            recv_sem=far_recv_sem.at[round_index, other ^ 1, face ^ 1],
            device_id=device,
            device_id_type=MESH,
        )

    def far_each(act):
        turns = [(a, b) for a in range(4) for b in range(4) if a // 2 != b // 2]
        for face, other in turns + [(a, a) for a in range(4)]:
            @pl.when(inside(*offset(face, other)))
            def _():
                act(face, other, place(*offset(face, other)))

    def far_start(round_index):
        far_each(lambda face, other, device: far_copy(round_index, face, other, device).start())

    def far_wait(round_index):
        far_each(
            lambda face, other, device: far_copy(
                round_index, other ^ 1, face ^ 1, device
            ).wait_recv()
        )

    def send_coarse(round_index, sem_row):
        for face in range(4):
            coarse_trace_to(w, owner[face], face, c_send.at[round_index, face])
        far_start(round_index)
        start_all(c_send, c_recv, round_index, sem_row)
        for face in range(4):
            far_recv[round_index, face, pl.ds(HALO * (face ^ 1), HALO), :] = c_send[
                round_index, face
            ]

    def send_ahead(round_index, sem_row):
        for face in range(4):
            coarse_trace_to(pre, owner[face], face, p_send.at[round_index, face])
        start_all(p_send, p_recv, round_index, sem_row)

    for e in range(SLOTS):
        loads["rhs", e].wait()
        live = jnp.where(e < counts[0], 1.0, 0.0)
        rhs[e] = rhs[e] * live
        loads["inv", e].wait()
        if e == 2:
            for name in late:
                loads[name].start()
        left_d[e] = pack_left(0.8 * inv_stage[e])
        v[e] = product(left_d[e], pack_right(rhs[e]))
    pl.semaphore_wait(barrier, peers)
    send_fine(0, 0)

    loads["lifts"].wait()
    loads["coefs"].wait()
    flat = pad_rows(jnp.concatenate([lifts[f] for f in range(6)], axis=0), 512)
    upright = jnp.transpose(pad_lanes(flat, 384))[:NF]
    lift_high, lift_low = halves(upright)
    lift_h[...] = lift_high
    lift_l[...] = lift_low
    coef_sq[...] = jnp.zeros((128, 128), f32)
    for f in range(6):
        coef_sq[pl.ds(8 * f, SLOTS), pl.ds(0, NFACE)] = coefs[f]
    columns = jnp.transpose(coef_sq[...])
    for e in range(SLOTS):
        for f in range(6):
            column = columns[:NFACE, 8 * f + e : 8 * f + e + 1]
            column = jnp.broadcast_to(column, (NFACE, RHS))
            coef_raw[e, f] = column
            coef_cols[e, f] = column * local[e, f].astype(f32)
    x_h[pl.ds(480, 32), :] = jnp.zeros((32, SLOTS * RHS), bf16)
    x_l[pl.ds(480, 32), :] = jnp.zeros((32, SLOTS * RHS), bf16)
    for e in range(SLOTS):
        loads["blocks", e].wait()
        left_a[e] = pack_left(stage[e])

    def local_residual():
        for e in range(SLOTS):
            for f in range(6):
                high, low = halves(coef_cols[e, f] * trace(v, slot[e, f], f ^ 1))
                x_h[pl.ds(NFACE * f, NFACE), pl.ds(RHS * e, RHS)] = high
                x_l[pl.ds(NFACE * f, NFACE), pl.ds(RHS * e, RHS)] = low
        for pair in range(2):
            cols = pl.ds(256 * pair, 256)
            coupled = (
                jnp.dot(lift_h[...], x_h[:, cols], preferred_element_type=f32)
                + jnp.dot(lift_h[...], x_l[:, cols], preferred_element_type=f32)
                + jnp.dot(lift_l[...], x_h[:, cols], preferred_element_type=f32)
            )
            for half in range(2):
                e = 2 * pair + half
                block = product(left_a[e], pack_right(v[e]))
                r_loc[e] = rhs[e] - block - coupled[:, 128 * half : 128 * half + 128]

    def presweep(which=range(SLOTS)):
        for e in which:
            vpre[e] = v[e] + product(left_d[e], pack_right(r_loc[e]))

    def cross_terms(left, recv):
        return [product(left[f], twice(recv[f], 128)) for f in range(4)]

    def combine(terms, src, dst):
        for e in range(SLOTS):
            total = src[e]
            for f in range(4):
                total = total - weight[e, f] * terms[f]
            dst[e] = total

    local_residual()
    presweep()
    scaled = []
    for f in range(4):
        coef_row = sum(weight[e, f] * coefs[f, pl.ds(e, 1), :] for e in range(SLOTS))
        square = jnp.transpose(pad_lanes(pad_rows(lifts[f], 128), 384))[:NF]
        scaled.append(square * pad_lanes(coef_row, 128))
    rights = [pack_right(s) for s in scaled]
    for f in range(4):
        high, low = halves(product(left_d[owner[f]], rights[f]))
        cross_l[f] = jnp.concatenate([high, low], axis=1)

    for face in range(4):
        f_send[1, face] = trace(vpre, owner[face], face)
    wait_all(f_send, f_recv, 0, 0)
    terms = cross_terms(cross_l, f_recv.at[0])
    for f in range(4):
        z[f] = terms[f]
    for face in range(4):
        line = f_send[1, face]
        for f in range(4):
            line = line - shared[face, f] * trace(z, f, face)
        f_send[1, face] = line
    start_all(f_send, f_recv, 1, 1)
    combine([z[f] for f in range(4)], vpre, v)

    local_residual()
    for name in ("cblocks", "cinv", "clifts", "ccoefs", "lift", "restrict", "face"):
        loads[name].wait()
    for e in range(SLOTS):
        left_ip[e] = pack_left(
            jnp.dot(0.2 * cinv[e], restrict_tab[...], precision=highest, preferred_element_type=f32)
        )
    for f in range(4):
        high, low = halves(product(left_ip[owner[f]], rights[f]))
        cross_k[f] = jnp.concatenate([high, low], axis=1)
    for e in range(SLOTS):
        w1[e] = product(left_ip[e], pack_right(r_loc[e]))
    clift_sq = [
        jnp.transpose(pad_lanes(pad_rows(clifts[f], 128), 128))[:NC] for f in range(6)
    ]

    def one_hot(rows, make):
        t = lax.broadcasted_iota(jnp.int32, (rows, 256), 0)
        lane = lax.broadcasted_iota(jnp.int32, (rows, 256), 1)
        return jnp.where(lane == make(t), 1.0, 0.0).astype(bf16)

    def face_target(e, f):
        def make(t):
            target = local[e, f] * (coarse_rows(f ^ 1, t) + 4 * HALO + NC * slot[e, f] + 1)
            if f < 4:
                target = target + cross[e, f] * (halo_rows(f, t) + HALO * f + 1)
            return jnp.where(t < NCF, target - 1, -1)

        return one_hot(32, make)

    def placed(matrix, chosen):
        high, low = halves(matrix)
        out = jnp.dot(
            jnp.concatenate([high, low], axis=0), chosen, preferred_element_type=f32
        )
        return out[:NC] + out[NC:]

    for e in range(SLOTS):
        start = 4 * HALO + NC * e
        total = placed(
            pad_lanes(cblocks[e], 128), one_hot(128, lambda t: jnp.where(t < NC, t + start, -1))
        )
        for f in range(6):
            scaled_lift = clift_sq[f] * pad_lanes(ccoefs[f, pl.ds(e, 1), :], 128)
            total = total + placed(scaled_lift[:, :32], face_target(e, f))
        row = lax.broadcasted_iota(jnp.int32, (NC, 256), 0)
        col = lax.broadcasted_iota(jnp.int32, (NC, 256), 1)
        unit = jnp.where(col == row + 4 * HALO + NC * e, 1.0, 0.0)
        full = unit - jnp.dot(
            0.8 * cinv[e], total, precision=highest, preferred_element_type=f32
        )
        coarse_m[e] = full
        coarse_h[e] = full[:, :128]
    for face in range(4):
        coarse_trace_to(coarse_h, owner[face], face, o_send.at[face])
        @pl.when(sides[face][0])
        def _():
            op_copy(face, face ^ 1).start()

    left_high, left_low = halves(coarse_m[...].reshape(SLOTS * NC, 256))
    left_m = jnp.concatenate([left_high, left_low], axis=0)
    presweep(range(2))

    wait_all(f_send, f_recv, 1, 1)
    combine(cross_terms(cross_k, f_recv.at[1]), w1, w)
    for e in range(SLOTS):
        w1[e] = w[e]
    send_coarse(0, 2)


    def quarters(left, right):
        high, low = halves(right)
        moved = jnp.dot(left, jnp.concatenate([high, low], axis=1), preferred_element_type=f32)
        rows = left.shape[0] // 2
        return moved[:rows, :128] + (moved[:rows, 128:] + moved[rows:, :128])

    def local_ahead(sem_row, round_index):
        state = jnp.concatenate(
            [jnp.zeros((4 * HALO, RHS), f32), w[...].reshape(SLOTS * NC, RHS)], axis=0
        )
        pre[...] = w1[...] + quarters(left_m, state).reshape(SLOTS, NC, RHS)
        send_ahead(round_index, sem_row)

    local_ahead(4, 0)
    for face in range(4):
        @pl.when(sides[face][0])
        def _():
            op_copy(face, face).wait_recv()
    blank = jnp.zeros((HALO, 128), f32)
    keep = lax.broadcasted_iota(jnp.int32, (HALO, 128), 1) < 4 * HALO
    op_rows = []
    for face in range(4):
        block = jnp.where(keep, o_recv[face], 0.0)
        op_rows.append(
            jnp.concatenate([block if k == face else blank for k in range(4)], axis=1)
        )
    op_full = jnp.concatenate(op_rows, axis=0)
    op_high, op_low = halves(op_full)
    op_left = jnp.concatenate([op_high, op_low], axis=0)

    def wide_product(left, right):
        high, low = halves(right)
        both = jnp.concatenate([high, low], axis=1)
        main, rest = both[:256], both[256:]
        out = jnp.dot(
            left,
            jnp.concatenate([main, main, rest, rest], axis=0),
            preferred_element_type=f32,
        )
        return out[:, :256] + out[:, 256:]

    def correction(pair):
        for half in range(2):
            e = 2 * pair + half
            for f in range(6):
                out = jnp.dot(
                    face_tab[:, :32], face_target(e, f), preferred_element_type=f32
                )
                coef = coef_raw[e, f]
                high, low = halves(
                    (out[:NFACE] + out[NFACE:]) * jnp.concatenate([coef, coef], axis=1)
                )
                x_h[pl.ds(NFACE * f, NFACE), pl.ds(256 * half, 256)] = high
                x_l[pl.ds(NFACE * f, NFACE), pl.ds(256 * half, 256)] = low
        for half in range(2):
            e = 2 * pair + half
            cols = pl.ds(256 * half, 256)
            start = 4 * HALO + NC * e
            coupled = (
                jnp.dot(lift_h[...], x_h[:, cols], preferred_element_type=f32)
                + jnp.dot(lift_h[...], x_l[:, cols], preferred_element_type=f32)
                + jnp.dot(lift_l[...], x_h[:, cols], preferred_element_type=f32)
            )
            chosen = one_hot(
                128, lambda t: jnp.where((t & 63) < NC, (t & 63) + start, -1)
            )
            prolonged = jnp.dot(lift_tab[...], chosen, preferred_element_type=f32)
            coupled = coupled + wide_product(left_a[e], prolonged)
            full = prolonged - wide_product(left_d[e], coupled)
            full_r[e] = full
            high, low = halves(full)
            left_r[e] = jnp.concatenate([high, low], axis=0)

    correction(0)
    presweep(range(2, SLOTS))

    def one_step(round_index, near_row, ahead_row):
        wait_all(c_send, c_recv, round_index, near_row)
        first = quarters(
            left_m[:, :128], pad_rows(c_recv[round_index].reshape(4 * HALO, RHS), 128)
        )
        middle = pre[...].reshape(SLOTS * NC, RHS) + first
        wait_all(p_send, p_recv, round_index, ahead_row)
        return jnp.concatenate([p_recv[round_index].reshape(4 * HALO, RHS), middle], axis=0)

    state = one_step(0, 2, 4)
    far_wait(0)
    halo = state[: 4 * HALO] + quarters(op_left, far_recv[0].reshape(512, RHS))
    ahead = quarters(left_m, jnp.concatenate([halo, state[4 * HALO :]], axis=0))
    w[...] = w1[...] + ahead.reshape(SLOTS, NC, RHS)
    send_coarse(1, 3)
    local_ahead(5, 1)
    correction(1)
    combine(cross_terms(cross_l, f_recv.at[1]), vpre, vpre)
    lines = [trace(full_r, owner[face], face) for face in range(4)]
    high, low = halves(jnp.concatenate(lines, axis=0))
    left_t = jnp.concatenate([high, low], axis=0)
    for face in range(4):
        f_send[2, face] = trace(vpre, owner[face], face)

    state = one_step(1, 3, 5)
    far_wait(1)
    halo = state[: 4 * HALO] + quarters(op_left, far_recv[1].reshape(512, RHS))
    high, low = halves(jnp.concatenate([halo, state[4 * HALO :]], axis=0))
    state = jnp.concatenate([high, low], axis=1)

    def moved_by(left):
        rows = left.shape[0] // 2
        moved = jnp.dot(left, state, preferred_element_type=f32)
        return moved[:rows, :128] + (moved[:rows, 128:] + moved[rows:, :128])

    moved = moved_by(left_t)
    for face in range(4):
        f_send[2, face] = f_send[2, face] + moved[NFACE * face : NFACE * face + NFACE]
    start_all(f_send, f_recv, 2, 6)
    for e in range(SLOTS):
        v[e] = vpre[e] + moved_by(left_r[e])
    local_residual()
    presweep()
    wait_all(f_send, f_recv, 2, 6)
    combine(cross_terms(cross_l, f_recv.at[2]), vpre, out)

    for face in range(4):
        @pl.when(sides[face][0])
        def _():
            for r, row in ((0, 0), (1, 1), (2, 6)):
                transfer(f_send, f_recv, r, row, face, face ^ 1).wait_send()
            for r in range(2):
                transfer(c_send, c_recv, r, 2 + r, face, face ^ 1).wait_send()
                transfer(p_send, p_recv, r, 4 + r, face, face ^ 1).wait_send()
            op_copy(face, face ^ 1).wait_send()
    for r in range(2):
        far_each(lambda face, other, device: far_copy(r, face, other, device).wait_send())


def body(*args):
    args = list(args)
    for i in (3, 7):
        args[i] = jnp.transpose(args[i], (0, 2, 1))
    for i in (4, 8):
        args[i] = jnp.transpose(args[i], (1, 0, 2))
    any_spec = pl.BlockSpec(memory_space=pltpu.HBM)
    constants = [jnp.asarray(c) for c in tables()]
    pin = lambda x: pltpu.with_memory_space_constraint(x, pltpu.HBM)
    args = [pin(a) for a in args[:10]] + args[10:]
    constants = [pin(c) for c in constants]
    vm = pltpu.VMEM
    scratch = [
        vm((SLOTS, NF, RHS), f32), vm((SLOTS, NF, NF), f32), vm((SLOTS, NF, NF), f32),
        vm((6, NFACE, NF), f32), vm((6, SLOTS, NFACE), f32),
        vm((SLOTS, NC, NC), f32), vm((SLOTS, NC, NC), f32), vm((6, NCF, NC), f32),
        vm((6, SLOTS, NCF), f32),
        vm((NF, 128), bf16), vm((NC, NF), f32), vm((2 * NFACE, 128), bf16),
        vm((SLOTS, NF, 640), bf16), vm((SLOTS, NF, 640), bf16),
        vm((NF, 512), bf16), vm((NF, 512), bf16),
        vm((SLOTS, 6, NFACE, RHS), f32), vm((128, 128), f32),
        vm((SLOTS, NF, RHS), f32), vm((SLOTS, NF, RHS), f32),
        vm((512, 512), bf16), vm((512, 512), bf16), vm((SLOTS, NF, RHS), f32),
        vm((4, NF, 256), bf16), vm((SLOTS, 2 * NF, 256), bf16), vm((SLOTS, NF, 256), f32), vm((SLOTS, 6, NFACE, RHS), f32), vm((4, NC, 256), bf16),
        vm((SLOTS, NC, 640), bf16), vm((SLOTS, NC, 256), f32),
        vm((SLOTS, NC, RHS), f32), vm((SLOTS, NC, RHS), f32),
        vm((4, NF, RHS), f32),
        vm((3, 4, NFACE, RHS), f32), vm((3, 4, NFACE, RHS), f32),
        vm((2, 4, HALO, RHS), f32), vm((2, 4, HALO, RHS), f32),
        vm((2, 4, 128, RHS), f32),
        vm((2, 4, HALO, RHS), f32), vm((2, 4, HALO, RHS), f32),
        vm((4, HALO, RHS), f32), vm((4, HALO, RHS), f32),
        vm((SLOTS, NC, 128), f32), vm((SLOTS, NC, RHS), f32),
        pltpu.SMEM((SLOTS, 6), jnp.int32),
        pltpu.SemaphoreType.DMA((24,)),
        pltpu.SemaphoreType.DMA((8, 4)), pltpu.SemaphoreType.DMA((8, 4)),
        pltpu.SemaphoreType.DMA((2, 4, 4)), pltpu.SemaphoreType.DMA((2, 4, 4)),
    ]
    return pl.pallas_call(
        kernel,
        out_shape=jax.ShapeDtypeStruct((SLOTS, NF, RHS), f32),
        in_specs=[any_spec] * 10 + [pl.BlockSpec(memory_space=pltpu.SMEM)] + [any_spec] * 3,
        out_specs=pl.BlockSpec(memory_space=pltpu.VMEM),
        scratch_shapes=scratch,
        compiler_params=pltpu.CompilerParams(collective_id=0, has_side_effects=True, vmem_limit_bytes=32 << 20),
        name="cycle",
    )(*args, *constants)


def solution(mesh):
    split = ("wide", "narrow")
    placed = (
        P(split, None, None),
        P(split, None, None),
        P(split, None, None),
        P(),
        P(split, None, None),
        P(split, None, None),
        P(split, None, None),
        P(),
        P(split, None, None),
        P(split, None),
        P(split),
    )
    return jax.shard_map(
        body, mesh=mesh, in_specs=placed, out_specs=P(split, None, None), check_vma=False
    )
```
